1024 devices in a mesh: pipe: 8 (over z), ctx: 16 (over x, core), head: 8 (over y).
Axes of the slice: x: 8, y: 8, z: 8, core: 2. Of those that a mesh axis runs over, the one named last changes fastest.
Arguments:
- queries: bfloat16 [8, 2048, 8192], P('pipe', 'ctx', 'head'), may hold values from -6 to 6
- key_states: bfloat16 [8, 2048, 1024], P('pipe', 'ctx', 'head'), may hold values from -6 to 6
- value_states: bfloat16 [8, 2048, 1024], P('pipe', 'ctx', 'head'), may hold values from -6 to 6
- upstream: bfloat16 [8, 2048, 8192], P('pipe', ('ctx', 'head')), may hold values from -6 to 6
- selected: int32 [8, 8, 32, 8], P('pipe', 'head', 'ctx'), may hold values from 0 to 31, as said below
Outputs:
- query_grad: bfloat16 [8, 2048, 8192], P('pipe', 'ctx', 'head')
- key_grad: bfloat16 [8, 2048, 1024], P('pipe', 'ctx', 'head')
- value_grad: bfloat16 [8, 2048, 1024], P('pipe', 'ctx', 'head')
The draws below stay inside these ranges and needn't reach their ends.
Inputs may be any that keep to these rules, and one draw needn't show every extreme that they name: `selected`: for query block b, entry 0 is b; the other 7 entries are distinct; min(b, 7) of them name blocks before b, the rest name blocks after b.
All inputs are finite; a program needn't handle non-finite values.
Results may differ from the reference program's by a relative error of at most 0.015.
Values may be sent and summed in bfloat16 or wider, within the bound.
A program may use at most 32 MiB of HBM per device.

```python
import jax
import jax.numpy as jnp
from jax import lax

QH = 64
KVH = 8
HD = 128
BLK = 64
TOPB = 8
SECTIONS = 8
TOKENS = 2048
QBLOCKS = 32
GROUP = 8


def draw_queries(key, part):
    own_key = jax.random.fold_in(key, 1)
    result = jnp.clip(jax.random.normal(own_key, (SECTIONS, TOKENS, QH * HD), jnp.float32), -6.0, 6.0)
    return result.astype(jnp.bfloat16)


def draw_key_states(key, part):
    own_key = jax.random.fold_in(key, 2)
    result = jnp.clip(jax.random.normal(own_key, (SECTIONS, TOKENS, KVH * HD), jnp.float32), -6.0, 6.0)
    return result.astype(jnp.bfloat16)


def draw_selected(key, part):
    own_key = jax.random.fold_in(key, 3)
    block_ids = jnp.arange(QBLOCKS, dtype=jnp.int32)
    earlier = block_ids[None, :] < block_ids[:, None]
    noise = jax.random.randint(own_key, (SECTIONS, KVH, QBLOCKS, QBLOCKS), 0, 1048576)
    ranking = jnp.where(earlier, noise * QBLOCKS + block_ids[None, :], block_ids[None, :] - 2 * QBLOCKS)
    picked = lax.top_k(ranking, TOPB - 1)[1].astype(jnp.int32)
    own_block = jnp.broadcast_to(block_ids[:, None], (SECTIONS, KVH, QBLOCKS, 1)).astype(jnp.int32)
    return jnp.concatenate([own_block, picked], axis=-1)


def shard_levels(key, dims, shards, smallest, high):
    gain, own = 1.0, jax.random.fold_in(key, 6)
    for axis_at, shards_of in shards:
        draws = jnp.exp(jax.random.uniform(jax.random.fold_in(own, axis_at), (shards_of,), jnp.float32, smallest / len(shards), high / len(shards)))
        gain = gain * jnp.repeat(draws, dims[axis_at] // shards_of).reshape([-1 if axis == axis_at else 1 for axis in range(len(dims))])
    return gain


def bell_draw(key, extent, width, bound, cuts=(), held_as=jnp.bfloat16):
    factor_of = shard_levels(key, extent, cuts, -0.22, 0.18) if cuts else 1.0
    values = jax.random.normal(key, extent, jnp.float32) * width * factor_of
    return jnp.minimum(jnp.maximum(values, -bound), bound).astype(held_as)


def setup_inputs(seed: int = 0) -> dict:
    arg_keys = jax.random.split(jax.random.key(seed), 6)
    queries = draw_queries(jax.random.fold_in(arg_keys[5], 71), 0)
    key_states = draw_key_states(jax.random.fold_in(arg_keys[5], 71), 0)
    value_states = bell_draw(arg_keys[2], (SECTIONS, TOKENS, KVH * HD), 1.0, 6.0, ((0, 8), (1, 16), (2, 8)))
    upstream = bell_draw(arg_keys[3], (SECTIONS, TOKENS, QH * HD), 1.0, 6.0, ((0, 8), (1, 128)))
    selected = draw_selected(jax.random.fold_in(arg_keys[5], 71), 0)
    return dict(queries=queries, key_states=key_states, value_states=value_states, upstream=upstream, selected=selected)


def section_grads(query_sec, key_sec, value_sec, grad_sec, chosen_sec):
    score_scale = HD ** -0.5
    query_tiles = query_sec.reshape(QBLOCKS, BLK, KVH, GROUP, HD)
    grad_tiles = grad_sec.reshape(QBLOCKS, BLK, KVH, GROUP, HD)
    key_table = key_sec.reshape(TOKENS, KVH, HD)
    value_table = value_sec.reshape(TOKENS, KVH, HD)
    offsets = jnp.arange(BLK, dtype=jnp.int32)
    head_index = jnp.arange(KVH, dtype=jnp.int32)[:, None]
    chosen = jnp.transpose(chosen_sec, (1, 0, 2))
    block_ids = jnp.arange(QBLOCKS, dtype=jnp.int32)

    def block_step(running, inputs):
        key_sums, value_sums = running
        query_blk, grad_blk, chosen_blk, block_index = inputs
        row_index = (chosen_blk[:, :, None] * BLK + offsets).reshape(KVH, TOPB * BLK)
        key_rows = key_table[row_index, head_index]
        value_rows = value_table[row_index, head_index]
        scores = jnp.einsum("icgh,cjh->cgij", query_blk.astype(jnp.float32), key_rows.astype(jnp.float32)) * score_scale
        query_pos = block_index * BLK + offsets
        visible = row_index[:, None, None, :] <= query_pos[None, None, :, None]
        scores = jnp.where(visible, scores, -jnp.inf)
        row_max = jnp.max(scores, axis=-1, keepdims=True)
        shifted = jnp.exp(scores - row_max)
        weights = shifted / jnp.sum(shifted, axis=-1, keepdims=True)
        weight_grad = jnp.einsum("icgh,cjh->cgij", grad_blk.astype(jnp.float32), value_rows.astype(jnp.float32))
        row_delta = jnp.sum(weights * weight_grad, axis=-1, keepdims=True)
        score_grad = (weights * (weight_grad - row_delta) * score_scale).astype(jnp.bfloat16)
        weight_half = weights.astype(jnp.bfloat16)
        query_part = jnp.einsum("cgij,cjh->icgh", score_grad.astype(jnp.float32), key_rows.astype(jnp.float32))
        key_part = jnp.einsum("cgij,icgh->cjh", score_grad.astype(jnp.float32), query_blk.astype(jnp.float32))
        value_part = jnp.einsum("cgij,icgh->cjh", weight_half.astype(jnp.float32), grad_blk.astype(jnp.float32))
        key_sums = key_sums.at[row_index, head_index].add(key_part)
        value_sums = value_sums.at[row_index, head_index].add(value_part)
        return (key_sums, value_sums), query_part.astype(jnp.bfloat16)

    start = (jnp.zeros((TOKENS, KVH, HD), jnp.float32), jnp.zeros((TOKENS, KVH, HD), jnp.float32))
    (key_sums, value_sums), query_parts = lax.scan(block_step, start, (query_tiles, grad_tiles, chosen, block_ids))
    query_grad = query_parts.reshape(TOKENS, QH * HD)
    key_grad = key_sums.reshape(TOKENS, KVH * HD).astype(jnp.bfloat16)
    value_grad = value_sums.reshape(TOKENS, KVH * HD).astype(jnp.bfloat16)
    return query_grad, key_grad, value_grad


def reference(queries, key_states, value_states, upstream, selected):
    out_grad = jnp.roll(upstream, -1, axis=0)

    def per_section(inputs):
        return section_grads(inputs[0], inputs[1], inputs[2], inputs[3], inputs[4])

    query_grad, key_grad, value_grad = lax.map(per_section, (queries, key_states, value_states, out_grad, selected))
    return query_grad, key_grad, value_grad
```

```python
import functools

import jax
import jax.numpy as jnp
from jax import lax
from jax.experimental import pallas as pl
from jax.experimental.pallas import tpu as pltpu
from jax.sharding import PartitionSpec as P

HD = 128
BLK = 64
GROUP = 8
TILE_HEADS = 4
SCALE = HD ** (-0.5)
LOG2E = 1.4426950408889634
HIDDEN = -1e30

NT_DIMS = (((1,), (1,)), ((), ()))
TN_DIMS = (((0,), (0,)), ((), ()))


def rows_of(index, size):
    return pl.ds(pl.multiple_of(index * size, size), size)


def body(sizes, tbl, q, k, v, up, dq_out, dk_out, dv_out, *scratch):
    pipes, ctxs, heads, tok, topb = sizes
    (
        kbuf, vbuf, qv, og, qs, os, ks, pf, pb, dsb, part_v, part_k,
        av, ak, sbv, sbk, rbv, rbk, gv, gk, hv, hk,
        loc_sem, up_send, up_recv,
        k_send, k_recv, k_fwd, k_sib, v_send, v_recv, v_fwd, v_sib,
        ev_send, ev_recv, ek_send, ek_recv,
        rv_send, rv_recv, rk_send, rk_recv,
    ) = scratch
    chips = ctxs // 2
    blocks = tok // BLK
    all_blocks = ctxs * blocks
    slots = topb + 1
    tiles = GROUP // TILE_HEADS
    width = GROUP * HD
    keys = topb * BLK
    up_rows = tok // heads
    hidden_at = blocks * topb
    slot_at = 2 * blocks * topb

    z = lax.axis_index("pipe")
    c = lax.axis_index("ctx")
    y = lax.axis_index("head")
    x = c // 2
    core = c % 2
    other = c + 1 - 2 * core
    z_prev = (z + pipes - 1) % pipes
    z_next = (z + 1) % pipes

    def blocks_of(owner):
        return pl.ds(owner * blocks, blocks)

    def at_chip(chip):
        return (z, chip * 2 + core, y)

    sibling = (z, other, y)

    def remote(src, dst, send, recv, target):
        return pltpu.make_async_remote_copy(
            src_ref=src, dst_ref=dst, send_sem=send, recv_sem=recv,
            device_id=target, device_id_type=pl.DeviceIdType.MESH,
        )

    q_copy = pltpu.make_async_copy(q.at[0], qv, loc_sem.at[0])
    k_copy = pltpu.make_async_copy(k, kbuf.at[blocks_of(c)], loc_sem.at[1])
    v_copy = pltpu.make_async_copy(v, vbuf.at[blocks_of(c)], loc_sem.at[2])
    q_copy.start()
    k_copy.start()
    v_copy.start()

    barrier = pltpu.get_barrier_semaphore()

    def greet(target):
        pl.semaphore_signal(barrier, inc=1, device_id=target, device_id_type=pl.DeviceIdType.MESH)

    greet(sibling)

    def greet_chip(d, carry):
        greet(at_chip((x + d) % chips))
        return carry

    def greet_head(h, carry):
        greet((z_next, c, h))
        return carry

    lax.fori_loop(1, chips, greet_chip, 0)
    lax.fori_loop(0, heads, greet_head, 0)

    zero_rows = jnp.zeros((BLK, HD), jnp.float32)
    for qb in range(blocks):
        part_v[qb * slots + topb] = zero_rows
        part_k[qb * slots + topb] = zero_rows

    pl.semaphore_wait(barrier, heads + chips)

    def gather_copy(src, buf, send, recv, chip, target):
        return remote(src, buf.at[blocks_of(c)], send.at[chip], recv.at[x], target)

    def send_keys(chip, carry):
        gather_copy(k, kbuf, k_send, k_recv, chip, at_chip(chip)).start()
        return carry

    def send_values(chip, carry):
        gather_copy(v, vbuf, v_send, v_recv, chip, at_chip(chip)).start()
        return carry

    def up_copy(h):
        return remote(
            up.at[0, :, rows_of(h, width)], og.at[rows_of(y, up_rows)],
            up_send.at[h], up_recv.at[y], (z_prev, c, h),
        )

    def send_up(h, carry):
        up_copy(h).start()
        return carry

    lax.fori_loop(x + 1, chips, send_keys, 0)
    gather_copy(k, kbuf, k_send, k_sib, x, sibling).start()
    lax.fori_loop(0, heads, send_up, 0)
    lax.fori_loop(x + 1, chips, send_values, 0)
    gather_copy(v, vbuf, v_send, v_sib, x, sibling).start()

    def passed_on(buf, fwd, sib, chip):
        block = buf.at[blocks_of(chip * 2 + core)]
        return remote(block, block, fwd.at[chip], sib.at[chip], sibling)

    def arrived(buf, recv, chip):
        block = buf.at[blocks_of(chip * 2 + core)]
        return remote(block, block, recv.at[chip], recv.at[chip], sibling)

    def from_sibling(buf, sib, chip):
        block = buf.at[blocks_of(chip * 2 + 1 - core)]
        return remote(block, block, sib.at[chip], sib.at[chip], sibling)

    def forward_all(buf, recv, fwd, sib):
        def step(i, carry):
            chip = x - 1 - i
            arrived(buf, recv, chip).wait_recv()
            passed_on(buf, fwd, sib, chip).start()
            return carry

        lax.fori_loop(0, x, step, 0)

    def wait_sibling(buf, sib):
        def step(chip, carry):
            from_sibling(buf, sib, chip).wait_recv()
            return carry

        lax.fori_loop(0, x + 1, step, 0)

    forward_all(kbuf, k_recv, k_fwd, k_sib)
    q_copy.wait()
    k_copy.wait()
    v_copy.wait()
    wait_sibling(kbuf, k_sib)

    def chosen_rows(buf, qb):
        return jnp.concatenate([buf[tbl[qb * topb + t]] for t in range(topb)], axis=0)

    def head_rows(ref, qb, tile):
        return jnp.concatenate(
            [ref[rows_of(qb, BLK), rows_of(tile * TILE_HEADS + h, HD)] for h in range(TILE_HEADS)],
            axis=0,
        )

    columns = TILE_HEADS * BLK

    def score_step(i, carry):
        qb, tile = i // tiles, i % tiles
        key_rows = chosen_rows(kbuf, qb)
        ks[qb] = key_rows
        query_rows = head_rows(qv, qb, tile)
        qs[i] = query_rows
        scores = lax.dot_general(key_rows, query_rows, NT_DIMS, preferred_element_type=jnp.float32)
        key_at = lax.broadcasted_iota(jnp.int32, (BLK, columns), 0)
        query_at = lax.broadcasted_iota(jnp.int32, (BLK, columns), 1) % BLK
        pieces = [jnp.where(key_at <= query_at, scores[:BLK], -jnp.inf)]
        for t in range(1, topb):
            shift = tbl[hidden_at + qb * topb + t].astype(jnp.float32) * HIDDEN
            pieces.append(scores[t * BLK:(t + 1) * BLK] + shift)
        scores = jnp.concatenate(pieces, axis=0)
        top = jnp.max(scores, axis=0, keepdims=True)
        weights = jnp.exp2((scores - top) * (SCALE * LOG2E))
        weights = weights * (1.0 / jnp.sum(weights, axis=0, keepdims=True))
        pf[i] = weights
        pb[i] = weights.astype(jnp.bfloat16)
        return carry

    lax.fori_loop(0, blocks * tiles, score_step, 0)

    forward_all(vbuf, v_recv, v_fwd, v_sib)

    def up_arrived(h, carry):
        block = og.at[rows_of(h, up_rows)]
        remote(block, block, up_recv.at[h], up_recv.at[h], sibling).wait_recv()
        return carry

    lax.fori_loop(0, heads, up_arrived, 0)

    def block_sums(lhs, rhs, part):
        def step(qb, carry):
            total = jnp.dot(lhs[qb * tiles], rhs[qb * tiles], preferred_element_type=jnp.float32)
            for tile in range(1, tiles):
                total += jnp.dot(
                    lhs[qb * tiles + tile], rhs[qb * tiles + tile], preferred_element_type=jnp.float32
                )
            for t in range(topb):
                part[qb * slots + t] = total[t * BLK:(t + 1) * BLK]
            return carry

        lax.fori_loop(0, blocks, step, 0)

    def grad_rows(i, carry):
        os[i] = head_rows(og, i // tiles, i % tiles)
        return carry

    lax.fori_loop(0, blocks * tiles, grad_rows, 0)
    block_sums(pb, os, part_v)

    def exchange_copy(src, dst, send, recv, chip):
        return remote(
            src.at[rows_of(chip, tok)], dst.at[rows_of(chip, tok)], send.at[chip], recv.at[chip], sibling
        )

    def exchange(part, own, out, landing, send, recv):
        def owner_block(owner, b):
            j = owner * blocks + b
            total = part[tbl[slot_at + j]]
            for qb in range(1, blocks):
                total = total + part[tbl[slot_at + qb * all_blocks + j]]
            return total

        def step(chip, carry):
            for b in range(blocks):
                at = rows_of(chip * blocks + b, BLK)
                out[at, :] = owner_block(chip * 2 + 1 - core, b).astype(jnp.bfloat16)
            exchange_copy(out, landing, send, recv, chip).start()
            for b in range(blocks):
                at = rows_of(chip * blocks + b, BLK)
                own[at, :] = owner_block(chip * 2 + core, b)
            return carry

        lax.fori_loop(0, x + 1, step, 0)

    exchange(part_v, av, sbv, rbv, ev_send, ev_recv)

    wait_sibling(vbuf, v_sib)

    def score_grad_step(i, carry):
        qb = i // tiles
        value_rows = chosen_rows(vbuf, qb)
        weight_grad = lax.dot_general(value_rows, os[i], NT_DIMS, preferred_element_type=jnp.float32)
        weights = pf[i]
        delta = jnp.sum(weights * weight_grad, axis=0, keepdims=True)
        dsb[i] = (weights * (weight_grad - delta) * SCALE).astype(jnp.bfloat16)
        return carry

    lax.fori_loop(0, blocks * tiles, score_grad_step, 0)

    def owner_copy(src, dst, send, recv, chip):
        return remote(src.at[rows_of(chip, tok)], dst.at[x], send.at[chip], recv.at[x], at_chip(chip))

    def send_owned(own, src, landing, out, owners, send, landed, rsend, rrecv):
        def step(i, carry):
            chip = x - 1 - i
            at = rows_of(chip, tok)
            exchange_copy(src, landing, send, landed, chip).wait_recv()
            out[at, :] = (own[at, :] + landing[at, :].astype(jnp.float32)).astype(jnp.bfloat16)
            owner_copy(out, owners, rsend, rrecv, chip).start()
            return carry

        lax.fori_loop(0, x, step, 0)
        at = rows_of(x, tok)
        exchange_copy(src, landing, send, landed, x).wait_recv()
        own[at, :] = own[at, :] + landing[at, :].astype(jnp.float32)

    send_owned(av, sbv, rbv, gv, hv, ev_send, ev_recv, rv_send, rv_recv)

    block_sums(dsb, qs, part_k)
    exchange(part_k, ak, sbk, rbk, ek_send, ek_recv)

    def query_step(i, carry):
        qb, tile = i // tiles, i % tiles
        grad = lax.dot_general(dsb[i], ks[qb], TN_DIMS, preferred_element_type=jnp.float32)
        grad = grad.astype(jnp.bfloat16)
        for h in range(TILE_HEADS):
            dq_out[0, rows_of(qb, BLK), rows_of(tile * TILE_HEADS + h, HD)] = grad[h * BLK:(h + 1) * BLK]
        return carry

    lax.fori_loop(0, blocks * tiles, query_step, 0)
    send_owned(ak, sbk, rbk, gk, hk, ek_send, ek_recv, rk_send, rk_recv)

    def owned_total(own, landing, recv, out):
        own_rows = own[rows_of(x, tok), :]

        def step(chip, total):
            block = landing.at[chip]
            remote(block, block, recv.at[chip], recv.at[chip], sibling).wait_recv()
            return total + landing[chip].astype(jnp.float32)

        out[0] = lax.fori_loop(x + 1, chips, step, own_rows).astype(jnp.bfloat16)

    owned_total(av, hv, rv_recv, dv_out)
    owned_total(ak, hk, rk_recv, dk_out)

    def left_gather(chip, carry):
        gather_copy(k, kbuf, k_send, k_recv, chip, at_chip(chip)).wait_send()
        gather_copy(v, vbuf, v_send, v_recv, chip, at_chip(chip)).wait_send()
        return carry

    def left_up(h, carry):
        up_copy(h).wait_send()
        return carry

    def left_lower(chip, carry):
        passed_on(kbuf, k_fwd, k_sib, chip).wait_send()
        passed_on(vbuf, v_fwd, v_sib, chip).wait_send()
        owner_copy(gv, hv, rv_send, rv_recv, chip).wait_send()
        owner_copy(gk, hk, rk_send, rk_recv, chip).wait_send()
        return carry

    def left_exchange(chip, carry):
        exchange_copy(sbv, rbv, ev_send, ev_recv, chip).wait_send()
        exchange_copy(sbk, rbk, ek_send, ek_recv, chip).wait_send()
        return carry

    lax.fori_loop(x, chips, left_gather, 0)
    lax.fori_loop(0, heads, left_up, 0)
    lax.fori_loop(0, x, left_lower, 0)
    lax.fori_loop(0, x + 1, left_exchange, 0)


def block_table(selected, ctxs, blocks):
    chosen = selected[0, 0]
    topb = chosen.shape[1]
    mine = lax.axis_index("ctx") * blocks + jnp.arange(blocks, dtype=jnp.int32)[:, None]
    slot = jnp.arange(topb, dtype=jnp.int32)
    every = jnp.arange(ctxs * blocks, dtype=jnp.int32)
    found = chosen[:, :, None] == every
    slots = topb + jnp.sum(jnp.where(found, slot[:, None] - topb, 0), axis=1)
    slots = slots + (topb + 1) * jnp.arange(blocks, dtype=jnp.int32)[:, None]
    hidden = (chosen > mine).astype(jnp.int32)
    return jnp.concatenate(
        [jnp.minimum(chosen, mine).reshape(-1), hidden.reshape(-1), slots.reshape(-1)]
    )


def per_device(pipes, ctxs, heads, queries, key_states, value_states, upstream, selected):
    tok = queries.shape[1]
    topb = selected.shape[3]
    blocks = tok // BLK
    chips = ctxs // 2
    tokens = tok * ctxs
    keys = topb * BLK
    tiles = GROUP // TILE_HEADS
    columns = TILE_HEADS * BLK
    width = GROUP * HD
    bf16, f32 = jnp.bfloat16, jnp.float32
    vmem = pltpu.VMEM
    dma = pltpu.SemaphoreType.DMA
    owned = (chips * tok, HD)
    scratch = [
        vmem((tokens // BLK, BLK, HD), bf16), vmem((tokens // BLK, BLK, HD), bf16),
        vmem((tok, width), bf16), vmem((tok, width), bf16),
        vmem((blocks * tiles, columns, HD), bf16), vmem((blocks * tiles, columns, HD), bf16),
        vmem((blocks, keys, HD), bf16),
        vmem((blocks * tiles, keys, columns), f32), vmem((blocks * tiles, keys, columns), bf16),
        vmem((blocks * tiles, keys, columns), bf16),
        vmem((blocks * (topb + 1), BLK, HD), f32), vmem((blocks * (topb + 1), BLK, HD), f32),
        vmem(owned, f32), vmem(owned, f32),
        vmem(owned, bf16), vmem(owned, bf16), vmem(owned, bf16), vmem(owned, bf16),
        vmem(owned, bf16), vmem(owned, bf16),
        vmem((chips, tok, HD), bf16), vmem((chips, tok, HD), bf16),
        dma((3,)), dma((heads,)), dma((heads,)),
    ] + [dma((chips,)) for _ in range(16)]
    sizes = (pipes, ctxs, heads, tok, topb)
    whole = pl.BlockSpec(memory_space=pltpu.VMEM)
    hbm = pl.BlockSpec(memory_space=pl.ANY)
    return pl.pallas_call(
        functools.partial(body, sizes),
        out_shape=(
            jax.ShapeDtypeStruct(queries.shape, bf16),
            jax.ShapeDtypeStruct(key_states.shape, bf16),
            jax.ShapeDtypeStruct(value_states.shape, bf16),
        ),
        in_specs=[pl.BlockSpec(memory_space=pltpu.SMEM), hbm, hbm, hbm, hbm],
        out_specs=(whole, whole, whole),
        scratch_shapes=scratch,
        compiler_params=pltpu.CompilerParams(
            collective_id=0, has_side_effects=True, vmem_limit_bytes=48 * 1024 * 1024
        ),
        name="selected_attention_grads",
    )(
        block_table(selected, ctxs, blocks),
        queries,
        key_states.reshape(blocks, BLK, HD),
        value_states.reshape(blocks, BLK, HD),
        upstream,
    )


def solution(mesh):
    placed = (
        P("pipe", "ctx", "head"),
        P("pipe", "ctx", "head"),
        P("pipe", "ctx", "head"),
        P("pipe", ("ctx", "head"), None),
        P("pipe", "head", "ctx", None),
    )
    per = functools.partial(per_device, mesh.shape["pipe"], mesh.shape["ctx"], mesh.shape["head"])
    return jax.shard_map(
        per,
        mesh=mesh,
        in_specs=placed,
        out_specs=(P("pipe", "ctx", "head"), P("pipe", "ctx", "head"), P("pipe", "ctx", "head")),
        check_vma=False,
    )
```

```python
import functools

import jax
import jax.numpy as jnp
from jax import lax
from jax.experimental import pallas as pl
from jax.experimental.pallas import tpu as pltpu
from jax.sharding import PartitionSpec as P

HD = 128
BLK = 64
GROUP = 8
TILE_HEADS = 4
SCALE = HD ** (-0.5)
LOG2E = 1.4426950408889634

NT_DIMS = (((1,), (1,)), ((), ()))
TN_DIMS = (((0,), (0,)), ((), ()))


def rows_of(index, size):
    return pl.ds(pl.multiple_of(index * size, size), size)


def body(sizes, sel_in, q, k, v, up, dq_out, dk_out, dv_out, *scratch):
    pipes, ctxs, heads, tok, topb = sizes
    (
        kbuf, vbuf, qv, og, qs, os, ks, pf, pb, dsb, part_v, part_k,
        av, ak, sbv, sbk, rbv, rbk, gv, gk, hv, hk, sel, tbl, ready,
        loc_sem, up_send, up_recv,
        k_send, k_recv, k_fwd, k_sib, v_send, v_recv, v_fwd, v_sib,
        ev_send, ev_recv, ek_send, ek_recv,
        rv_send, rv_recv, rk_send, rk_recv,
    ) = scratch
    chips = ctxs // 2
    blocks = tok // BLK
    all_blocks = ctxs * blocks
    slots = topb + 1
    tiles = GROUP // TILE_HEADS
    width = GROUP * HD
    keys = topb * BLK
    up_rows = tok // heads

    z = lax.axis_index("pipe")
    c = lax.axis_index("ctx")
    y = lax.axis_index("head")
    x = c // 2
    core = c % 2
    other = c + 1 - 2 * core
    z_prev = (z + pipes - 1) % pipes
    z_next = (z + 1) % pipes

    def blocks_of(owner):
        return pl.ds(owner * blocks, blocks)

    def at_chip(chip):
        return (z, chip * 2 + core, y)

    sibling = (z, other, y)

    def remote(src, dst, send, recv, target):
        return pltpu.make_async_remote_copy(
            src_ref=src, dst_ref=dst, send_sem=send, recv_sem=recv,
            device_id=target, device_id_type=pl.DeviceIdType.MESH,
        )

    q_copy = pltpu.make_async_copy(q.at[0], qv, loc_sem.at[0])
    k_copy = pltpu.make_async_copy(k, kbuf.at[blocks_of(c)], loc_sem.at[1])
    v_copy = pltpu.make_async_copy(v, vbuf.at[blocks_of(c)], loc_sem.at[2])
    sel_copy = pltpu.make_async_copy(sel_in, sel, loc_sem.at[3])
    sel_copy.start()
    q_copy.start()
    k_copy.start()
    v_copy.start()

    barrier = pltpu.get_barrier_semaphore()

    def greet(semaphore, target):
        pl.semaphore_signal(semaphore, inc=1, device_id=target, device_id_type=pl.DeviceIdType.MESH)

    greet(barrier, sibling)

    def greet_chip(d, carry):
        greet(barrier, at_chip((x + d) % chips))
        return carry

    def greet_receiver(h, carry):
        greet(barrier, (z_prev, c, h))
        return carry

    def greet_sender(h, carry):
        greet(ready, (z_next, c, h))
        return carry

    lax.fori_loop(1, chips, greet_chip, 0)
    lax.fori_loop(0, heads, greet_receiver, 0)
    pl.semaphore_wait(barrier, heads + chips)

    def gather_copy(src, buf, send, recv, chip, target):
        return remote(src, buf.at[blocks_of(c)], send.at[chip], recv.at[x], target)

    def send_keys(chip, carry):
        gather_copy(k, kbuf, k_send, k_recv, chip, at_chip(chip)).start()
        return carry

    def send_values(chip, carry):
        gather_copy(v, vbuf, v_send, v_recv, chip, at_chip(chip)).start()
        return carry

    def up_copy(h):
        return remote(
            up.at[0, :, rows_of(h, width)], og.at[rows_of(y, up_rows)],
            up_send.at[h], up_recv.at[y], (z_prev, c, h),
        )

    def send_up(h, carry):
        up_copy(h).start()
        return carry

    lax.fori_loop(x + 1, chips, send_keys, 0)
    gather_copy(k, kbuf, k_send, k_sib, x, sibling).start()
    lax.fori_loop(0, heads, greet_sender, 0)
    lax.fori_loop(x + 1, chips, send_values, 0)
    gather_copy(v, vbuf, v_send, v_sib, x, sibling).start()

    def send_all_up():
        pl.semaphore_wait(ready, heads)
        lax.fori_loop(0, heads, send_up, 0)

    @pl.when(z > 0)
    def _():
        send_all_up()

    sel_copy.wait()

    def slot_row(j, carry):
        for qb in range(blocks):
            slot = jnp.int32(topb)
            for t in range(topb):
                slot = jnp.where(sel[0, 0, qb, t] == j, jnp.int32(t), slot)
            tbl[qb * all_blocks + j] = slot + qb * slots
        return carry

    lax.fori_loop(0, all_blocks, slot_row, 0)
    zero_rows = jnp.zeros((BLK, HD), jnp.float32)
    for qb in range(blocks):
        part_v[qb * slots + topb] = zero_rows
        part_k[qb * slots + topb] = zero_rows

    def passed_on(buf, fwd, sib, chip):
        block = buf.at[blocks_of(chip * 2 + core)]
        return remote(block, block, fwd.at[chip], sib.at[chip], sibling)

    def arrived(buf, recv, chip):
        block = buf.at[blocks_of(chip * 2 + core)]
        return remote(block, block, recv.at[chip], recv.at[chip], sibling)

    def from_sibling(buf, sib, chip):
        block = buf.at[blocks_of(chip * 2 + 1 - core)]
        return remote(block, block, sib.at[chip], sib.at[chip], sibling)

    def forward_all(buf, recv, fwd, sib):
        def step(i, carry):
            chip = x - 1 - i
            arrived(buf, recv, chip).wait_recv()
            passed_on(buf, fwd, sib, chip).start()
            return carry

        lax.fori_loop(0, x, step, 0)

    def wait_sibling(buf, sib):
        def step(chip, carry):
            from_sibling(buf, sib, chip).wait_recv()
            return carry

        lax.fori_loop(0, x + 1, step, 0)

    forward_all(kbuf, k_recv, k_fwd, k_sib)
    q_copy.wait()
    k_copy.wait()
    v_copy.wait()
    wait_sibling(kbuf, k_sib)

    def chosen_rows(buf, qb):
        mine = c * blocks + qb
        return jnp.concatenate(
            [buf[jnp.minimum(sel[0, 0, qb, t], mine)] for t in range(topb)], axis=0
        )

    def head_rows(ref, qb, tile):
        return jnp.concatenate(
            [ref[rows_of(qb, BLK), rows_of(tile * TILE_HEADS + h, HD)] for h in range(TILE_HEADS)],
            axis=0,
        )

    columns = TILE_HEADS * BLK

    def score_step(i, carry):
        qb, tile = i // tiles, i % tiles
        mine = c * blocks + qb
        key_rows = chosen_rows(kbuf, qb)
        ks[qb] = key_rows
        query_rows = head_rows(qv, qb, tile)
        qs[i] = query_rows
        scores = lax.dot_general(key_rows, query_rows, NT_DIMS, preferred_element_type=jnp.float32)
        key_at = lax.broadcasted_iota(jnp.int32, (BLK, columns), 0)
        query_at = lax.broadcasted_iota(jnp.int32, (BLK, columns), 1) % BLK
        pieces = [jnp.where(key_at <= query_at, scores[:BLK], -jnp.inf)]
        for t in range(1, topb):
            shift = jnp.where(sel[0, 0, qb, t] > mine, jnp.float32(-jnp.inf), jnp.float32(0.0))
            pieces.append(scores[t * BLK:(t + 1) * BLK] + shift)
        scores = jnp.concatenate(pieces, axis=0)
        top = jnp.max(scores, axis=0, keepdims=True)
        weights = jnp.exp2((scores - top) * (SCALE * LOG2E))
        weights = weights * (1.0 / jnp.sum(weights, axis=0, keepdims=True))
        pf[i] = weights
        pb[i] = weights.astype(jnp.bfloat16)
        return carry

    lax.fori_loop(0, blocks * tiles, score_step, 0)

    @pl.when(z == 0)
    def _():
        send_all_up()


    forward_all(vbuf, v_recv, v_fwd, v_sib)

    def up_arrived(h, carry):
        block = og.at[rows_of(h, up_rows)]
        remote(block, block, up_recv.at[h], up_recv.at[h], sibling).wait_recv()
        return carry

    lax.fori_loop(0, heads, up_arrived, 0)

    def block_sums(lhs, rhs, part):
        def step(qb, carry):
            total = jnp.dot(lhs[qb * tiles], rhs[qb * tiles], preferred_element_type=jnp.float32)
            for tile in range(1, tiles):
                total += jnp.dot(
                    lhs[qb * tiles + tile], rhs[qb * tiles + tile], preferred_element_type=jnp.float32
                )
            for t in range(topb):
                part[qb * slots + t] = total[t * BLK:(t + 1) * BLK]
            return carry

        lax.fori_loop(0, blocks, step, 0)

    def grad_rows(i, carry):
        os[i] = head_rows(og, i // tiles, i % tiles)
        return carry

    lax.fori_loop(0, blocks * tiles, grad_rows, 0)
    block_sums(pb, os, part_v)

    def exchange_copy(src, dst, send, recv, chip):
        return remote(
            src.at[rows_of(chip, tok)], dst.at[rows_of(chip, tok)], send.at[chip], recv.at[chip], sibling
        )

    def exchange(part, own, out, landing, send, recv):
        def owner_block(owner, b):
            j = owner * blocks + b
            total = part[tbl[j]]
            for qb in range(1, blocks):
                total = total + part[tbl[qb * all_blocks + j]]
            return total

        def step(chip, carry):
            for b in range(blocks):
                at = rows_of(chip * blocks + b, BLK)
                out[at, :] = owner_block(chip * 2 + 1 - core, b).astype(jnp.bfloat16)
            exchange_copy(out, landing, send, recv, chip).start()
            for b in range(blocks):
                at = rows_of(chip * blocks + b, BLK)
                own[at, :] = owner_block(chip * 2 + core, b)
            return carry

        lax.fori_loop(0, x + 1, step, 0)

    exchange(part_v, av, sbv, rbv, ev_send, ev_recv)

    wait_sibling(vbuf, v_sib)

    def score_grad_step(i, carry):
        qb = i // tiles
        value_rows = chosen_rows(vbuf, qb)
        weight_grad = lax.dot_general(value_rows, os[i], NT_DIMS, preferred_element_type=jnp.float32)
        weights = pf[i]
        delta = jnp.sum(weights * weight_grad, axis=0, keepdims=True)
        dsb[i] = (weights * (weight_grad - delta) * SCALE).astype(jnp.bfloat16)
        return carry

    lax.fori_loop(0, blocks * tiles, score_grad_step, 0)

    def owner_copy(src, dst, send, recv, chip):
        return remote(src.at[rows_of(chip, tok)], dst.at[x], send.at[chip], recv.at[x], at_chip(chip))

    def send_owned(own, src, landing, out, owners, send, landed, rsend, rrecv):
        def step(i, carry):
            chip = x - 1 - i
            at = rows_of(chip, tok)
            exchange_copy(src, landing, send, landed, chip).wait_recv()
            out[at, :] = (own[at, :] + landing[at, :].astype(jnp.float32)).astype(jnp.bfloat16)
            owner_copy(out, owners, rsend, rrecv, chip).start()
            return carry

        lax.fori_loop(0, x, step, 0)
        at = rows_of(x, tok)
        exchange_copy(src, landing, send, landed, x).wait_recv()
        own[at, :] = own[at, :] + landing[at, :].astype(jnp.float32)

    send_owned(av, sbv, rbv, gv, hv, ev_send, ev_recv, rv_send, rv_recv)

    block_sums(dsb, qs, part_k)
    exchange(part_k, ak, sbk, rbk, ek_send, ek_recv)

    def query_step(i, carry):
        qb, tile = i // tiles, i % tiles
        grad = lax.dot_general(dsb[i], ks[qb], TN_DIMS, preferred_element_type=jnp.float32)
        grad = grad.astype(jnp.bfloat16)
        for h in range(TILE_HEADS):
            dq_out[0, rows_of(qb, BLK), rows_of(tile * TILE_HEADS + h, HD)] = grad[h * BLK:(h + 1) * BLK]
        return carry

    lax.fori_loop(0, blocks * tiles, query_step, 0)
    send_owned(ak, sbk, rbk, gk, hk, ek_send, ek_recv, rk_send, rk_recv)

    def owned_total(own, landing, recv, out):
        own_rows = own[rows_of(x, tok), :]

        def step(chip, total):
            block = landing.at[chip]
            remote(block, block, recv.at[chip], recv.at[chip], sibling).wait_recv()
            return total + landing[chip].astype(jnp.float32)

        out[0] = lax.fori_loop(x + 1, chips, step, own_rows).astype(jnp.bfloat16)

    owned_total(av, hv, rv_recv, dv_out)
    owned_total(ak, hk, rk_recv, dk_out)

    def left_gather(chip, carry):
        gather_copy(k, kbuf, k_send, k_recv, chip, at_chip(chip)).wait_send()
        gather_copy(v, vbuf, v_send, v_recv, chip, at_chip(chip)).wait_send()
        return carry

    def left_up(h, carry):
        up_copy(h).wait_send()
        return carry

    def left_lower(chip, carry):
        passed_on(kbuf, k_fwd, k_sib, chip).wait_send()
        passed_on(vbuf, v_fwd, v_sib, chip).wait_send()
        owner_copy(gv, hv, rv_send, rv_recv, chip).wait_send()
        owner_copy(gk, hk, rk_send, rk_recv, chip).wait_send()
        return carry

    def left_exchange(chip, carry):
        exchange_copy(sbv, rbv, ev_send, ev_recv, chip).wait_send()
        exchange_copy(sbk, rbk, ek_send, ek_recv, chip).wait_send()
        return carry

    lax.fori_loop(x, chips, left_gather, 0)
    lax.fori_loop(0, heads, left_up, 0)
    lax.fori_loop(0, x, left_lower, 0)
    lax.fori_loop(0, x + 1, left_exchange, 0)


def per_device(pipes, ctxs, heads, queries, key_states, value_states, upstream, selected):
    tok = queries.shape[1]
    topb = selected.shape[3]
    blocks = tok // BLK
    chips = ctxs // 2
    tokens = tok * ctxs
    keys = topb * BLK
    tiles = GROUP // TILE_HEADS
    columns = TILE_HEADS * BLK
    width = GROUP * HD
    bf16, f32 = jnp.bfloat16, jnp.float32
    vmem = pltpu.VMEM
    dma = pltpu.SemaphoreType.DMA
    owned = (chips * tok, HD)
    scratch = [
        vmem((tokens // BLK, BLK, HD), bf16), vmem((tokens // BLK, BLK, HD), bf16),
        vmem((tok, width), bf16), vmem((tok, width), bf16),
        vmem((blocks * tiles, columns, HD), bf16), vmem((blocks * tiles, columns, HD), bf16),
        vmem((blocks, keys, HD), bf16),
        vmem((blocks * tiles, keys, columns), f32), vmem((blocks * tiles, keys, columns), bf16),
        vmem((blocks * tiles, keys, columns), bf16),
        vmem((blocks * (topb + 1), BLK, HD), f32), vmem((blocks * (topb + 1), BLK, HD), f32),
        vmem(owned, f32), vmem(owned, f32),
        vmem(owned, bf16), vmem(owned, bf16), vmem(owned, bf16), vmem(owned, bf16),
        vmem(owned, bf16), vmem(owned, bf16),
        vmem((chips, tok, HD), bf16), vmem((chips, tok, HD), bf16),
        pltpu.SMEM((1, 1, blocks, topb), jnp.int32),
        pltpu.SMEM((blocks * ctxs * blocks,), jnp.int32),
        pltpu.SemaphoreType.REGULAR,
        dma((4,)), dma((heads,)), dma((heads,)),
    ] + [dma((chips,)) for _ in range(16)]
    sizes = (pipes, ctxs, heads, tok, topb)
    whole = pl.BlockSpec(memory_space=pltpu.VMEM)
    hbm = pl.BlockSpec(memory_space=pltpu.HBM)
    return pl.pallas_call(
        functools.partial(body, sizes),
        out_shape=(
            jax.ShapeDtypeStruct(queries.shape, bf16),
            jax.ShapeDtypeStruct(key_states.shape, bf16),
            jax.ShapeDtypeStruct(value_states.shape, bf16),
        ),
        in_specs=[hbm] * 5,
        out_specs=(whole, whole, whole),
        scratch_shapes=scratch,
        compiler_params=pltpu.CompilerParams(
            collective_id=0, has_side_effects=True, vmem_limit_bytes=48 * 1024 * 1024
        ),
        name="selected_attention_grads",
    )(
        selected,
        queries,
        key_states.reshape(blocks, BLK, HD),
        value_states.reshape(blocks, BLK, HD),
        upstream,
    )


def solution(mesh):
    placed = (
        P("pipe", "ctx", "head"),
        P("pipe", "ctx", "head"),
        P("pipe", "ctx", "head"),
        P("pipe", ("ctx", "head"), None),
        P("pipe", "head", "ctx", None),
    )
    per = functools.partial(per_device, mesh.shape["pipe"], mesh.shape["ctx"], mesh.shape["head"])
    return jax.shard_map(
        per,
        mesh=mesh,
        in_specs=placed,
        out_specs=(P("pipe", "ctx", "head"), P("pipe", "ctx", "head"), P("pipe", "ctx", "head")),
        check_vma=False,
    )
```

```python
import functools

import jax
import jax.numpy as jnp
from jax import lax
from jax.experimental import pallas as pl
from jax.experimental.pallas import tpu as pltpu
from jax.sharding import PartitionSpec as P

HD = 128
BLK = 64
GROUP = 8
TILE_HEADS = 4
SCALE = HD ** (-0.5)
LOG2E = 1.4426950408889634

NT_DIMS = (((1,), (1,)), ((), ()))
TN_DIMS = (((0,), (0,)), ((), ()))


def rows_of(index, size):
    return pl.ds(pl.multiple_of(index * size, size), size)


def body(sizes, sel_in, q, k, v, up, dq_out, dk_out, dv_out, *scratch):
    pipes, ctxs, heads, tok, topb = sizes
    (
        kbuf, vbuf, qv, og, qs, os, ks, pf, pb, dsb, part_v, part_k,
        av, ak, sbv, sbk, rbv, rbk, gv, gk, hv, hk, dq, dkv, sel, tbl, ready,
        loc_sem, up_send, up_recv,
        k_send, k_recv, k_fwd, k_sib, v_send, v_recv, v_fwd, v_sib,
        ev_send, ev_recv, ek_send, ek_recv,
        rv_send, rv_recv, rk_send, rk_recv,
    ) = scratch
    chips = ctxs // 2
    blocks = tok // BLK
    all_blocks = ctxs * blocks
    slots = topb + 1
    tiles = GROUP // TILE_HEADS
    width = GROUP * HD
    keys = topb * BLK
    up_rows = tok // heads

    z = lax.axis_index("pipe")
    c = lax.axis_index("ctx")
    y = lax.axis_index("head")
    x = c // 2
    core = c % 2
    other = c + 1 - 2 * core
    z_prev = (z + pipes - 1) % pipes
    z_next = (z + 1) % pipes

    def blocks_of(owner):
        return pl.ds(owner * blocks, blocks)

    def at_chip(chip):
        return (z, chip * 2 + core, y)

    sibling = (z, other, y)

    def remote(src, dst, send, recv, target):
        return pltpu.make_async_remote_copy(
            src_ref=src, dst_ref=dst, send_sem=send, recv_sem=recv,
            device_id=target, device_id_type=pl.DeviceIdType.MESH,
        )

    q_copy = pltpu.make_async_copy(q.at[0], qv, loc_sem.at[0])
    k_copy = pltpu.make_async_copy(k, kbuf.at[blocks_of(c)], loc_sem.at[1])
    v_copy = pltpu.make_async_copy(v, vbuf.at[blocks_of(c)], loc_sem.at[2])
    sel_copy = pltpu.make_async_copy(sel_in, sel, loc_sem.at[3])
    sel_copy.start()
    q_copy.start()
    k_copy.start()
    v_copy.start()

    barrier = pltpu.get_barrier_semaphore()

    def told_later(section):
        return jnp.logical_or(section == 0, jnp.logical_and(section == 1, c == 0))

    def as_int(flag):
        return jnp.where(flag, jnp.int32(1), jnp.int32(0))

    late = told_later(z)
    next_late = told_later(z_next)

    def greet(semaphore, target):
        pl.semaphore_signal(semaphore, inc=1, device_id=target, device_id_type=pl.DeviceIdType.MESH)

    def greet_chip(chip, carry):
        greet(barrier, at_chip(chip))
        return carry

    def greet_receiver(h, carry):
        greet(barrier, (z_prev, c, h))
        return carry

    def greet_sender(h, carry):
        greet(barrier, (z_next, c, h))
        return carry

    def tell_sender(h, carry):
        greet(ready, (z_next, c, h))
        return carry

    lax.fori_loop(0, x, greet_chip, 0)

    @pl.when(core == 1)
    def _():
        greet(barrier, sibling)

    @pl.when(jnp.logical_not(next_late))
    def _():
        lax.fori_loop(0, heads, greet_sender, 0)

    @pl.when(late)
    def _():
        lax.fori_loop(0, heads, greet_receiver, 0)

    expected = chips - 1 - x + (1 - core) + heads * (1 - as_int(late)) + heads * as_int(next_late)

    @pl.when(expected > 0)
    def _():
        pl.semaphore_wait(barrier, expected)

    def gather_copy(src, buf, send, recv, chip, target):
        return remote(src, buf.at[blocks_of(c)], send.at[chip], recv.at[x], target)

    def send_keys(chip, carry):
        gather_copy(k, kbuf, k_send, k_recv, chip, at_chip(chip)).start()
        return carry

    def send_values(chip, carry):
        gather_copy(v, vbuf, v_send, v_recv, chip, at_chip(chip)).start()
        return carry

    def send_to_sibling():
        gather_copy(k, kbuf, k_send, k_sib, x, sibling).start()
        gather_copy(v, vbuf, v_send, v_sib, x, sibling).start()

    def up_copy(h):
        return remote(
            up.at[0, :, rows_of(h, width)], og.at[rows_of(y, up_rows)],
            up_send.at[h], up_recv.at[y], (z_prev, c, h),
        )

    def send_up(h, carry):
        up_copy(h).start()
        return carry

    lax.fori_loop(x + 1, chips, send_keys, 0)

    @pl.when(core == 0)
    def _():
        send_to_sibling()

    lax.fori_loop(x + 1, chips, send_values, 0)

    @pl.when(next_late)
    def _():
        lax.fori_loop(0, heads, tell_sender, 0)

    @pl.when(jnp.logical_not(late))
    def _():
        lax.fori_loop(0, heads, send_up, 0)

    sel_copy.wait()

    def slot_row(j, carry):
        for qb in range(blocks):
            slot = jnp.int32(topb)
            for t in range(topb):
                slot = jnp.where(sel[0, 0, qb, t] == j, jnp.int32(t), slot)
            tbl[qb * all_blocks + j] = slot + qb * slots
        return carry

    lax.fori_loop(0, all_blocks, slot_row, 0)
    zero_rows = jnp.zeros((BLK, HD), jnp.float32)
    for qb in range(blocks):
        part_v[qb * slots + topb] = zero_rows
        part_k[qb * slots + topb] = zero_rows

    def passed_on(buf, fwd, sib, chip):
        block = buf.at[blocks_of(chip * 2 + core)]
        return remote(block, block, fwd.at[chip], sib.at[chip], sibling)

    def arrived(buf, recv, chip):
        block = buf.at[blocks_of(chip * 2 + core)]
        return remote(block, block, recv.at[chip], recv.at[chip], sibling)

    def from_sibling(buf, sib, chip):
        block = buf.at[blocks_of(chip * 2 + 1 - core)]
        return remote(block, block, sib.at[chip], sib.at[chip], sibling)

    def forward_all(buf, recv, fwd, sib):
        def step(i, carry):
            chip = x - 1 - i
            arrived(buf, recv, chip).wait_recv()
            passed_on(buf, fwd, sib, chip).start()
            return carry

        lax.fori_loop(0, x, step, 0)

    def wait_sibling(buf, sib, count):
        def step(chip, carry):
            from_sibling(buf, sib, chip).wait_recv()
            return carry

        lax.fori_loop(0, count, step, 0)

    @pl.when(core == 1)
    def _():
        from_sibling(kbuf, k_sib, x).wait_recv()
        send_to_sibling()

    forward_all(kbuf, k_recv, k_fwd, k_sib)
    q_copy.wait()
    k_copy.wait()
    v_copy.wait()
    wait_sibling(kbuf, k_sib, x + 1 - core)

    def chosen_rows(buf, qb):
        mine = c * blocks + qb
        return jnp.concatenate(
            [buf[jnp.minimum(sel[0, 0, qb, t], mine)] for t in range(topb)], axis=0
        )

    def head_rows(ref, qb, tile):
        return jnp.concatenate(
            [ref[rows_of(qb, BLK), rows_of(tile * TILE_HEADS + h, HD)] for h in range(TILE_HEADS)],
            axis=0,
        )

    columns = TILE_HEADS * BLK

    def score_step(i, carry):
        qb, tile = i // tiles, i % tiles
        mine = c * blocks + qb
        key_rows = chosen_rows(kbuf, qb)
        ks[qb] = key_rows
        query_rows = head_rows(qv, qb, tile)
        qs[i] = query_rows
        scores = lax.dot_general(key_rows, query_rows, NT_DIMS, preferred_element_type=jnp.float32)
        key_at = lax.broadcasted_iota(jnp.int32, (BLK, columns), 0)
        query_at = lax.broadcasted_iota(jnp.int32, (BLK, columns), 1) % BLK
        pieces = [jnp.where(key_at <= query_at, scores[:BLK], -jnp.inf)]
        for t in range(1, topb):
            shift = jnp.where(sel[0, 0, qb, t] > mine, jnp.float32(-jnp.inf), jnp.float32(0.0))
            pieces.append(scores[t * BLK:(t + 1) * BLK] + shift)
        scores = jnp.concatenate(pieces, axis=0)
        top = jnp.max(scores, axis=0, keepdims=True)
        weights = jnp.exp2((scores - top) * (SCALE * LOG2E))
        weights = weights * (1.0 / jnp.sum(weights, axis=0, keepdims=True))
        pf[i] = weights
        pb[i] = weights.astype(jnp.bfloat16)
        return carry

    lax.fori_loop(0, blocks * tiles, score_step, 0)

    forward_all(vbuf, v_recv, v_fwd, v_sib)

    def up_arrived(h, carry):
        block = og.at[rows_of(h, up_rows)]
        remote(block, block, up_recv.at[h], up_recv.at[h], sibling).wait_recv()
        return carry

    lax.fori_loop(0, heads, up_arrived, 0)

    def block_sums(lhs, rhs, part):
        def step(qb, carry):
            total = jnp.dot(lhs[qb * tiles], rhs[qb * tiles], preferred_element_type=jnp.float32)
            for tile in range(1, tiles):
                total += jnp.dot(
                    lhs[qb * tiles + tile], rhs[qb * tiles + tile], preferred_element_type=jnp.float32
                )
            for t in range(topb):
                part[qb * slots + t] = total[t * BLK:(t + 1) * BLK]
            return carry

        lax.fori_loop(0, blocks, step, 0)

    def grad_rows(i, carry):
        os[i] = head_rows(og, i // tiles, i % tiles)
        return carry

    lax.fori_loop(0, blocks * tiles, grad_rows, 0)
    block_sums(pb, os, part_v)

    def exchange_copy(src, dst, send, recv, chip):
        return remote(
            src.at[rows_of(chip, tok)], dst.at[rows_of(chip, tok)], send.at[chip], recv.at[chip], sibling
        )

    def exchange(part, own, out, landing, send, recv):
        def owner_block(owner, b):
            j = owner * blocks + b
            total = part[tbl[j]]
            for qb in range(1, blocks):
                total = total + part[tbl[qb * all_blocks + j]]
            return total

        def step(chip, carry):
            for b in range(blocks):
                at = rows_of(chip * blocks + b, BLK)
                out[at, :] = owner_block(chip * 2 + 1 - core, b).astype(jnp.bfloat16)
            exchange_copy(out, landing, send, recv, chip).start()
            for b in range(blocks):
                at = rows_of(chip * blocks + b, BLK)
                own[at, :] = owner_block(chip * 2 + core, b)
            return carry

        lax.fori_loop(0, x + 1, step, 0)

    exchange(part_v, av, sbv, rbv, ev_send, ev_recv)

    wait_sibling(vbuf, v_sib, x + 1)

    def score_grad_step(i, carry):
        qb = i // tiles
        value_rows = chosen_rows(vbuf, qb)
        weight_grad = lax.dot_general(value_rows, os[i], NT_DIMS, preferred_element_type=jnp.float32)
        weights = pf[i]
        delta = jnp.sum(weights * weight_grad, axis=0, keepdims=True)
        dsb[i] = (weights * (weight_grad - delta) * SCALE).astype(jnp.bfloat16)
        return carry

    lax.fori_loop(0, blocks * tiles, score_grad_step, 0)

    def owner_copy(src, dst, send, recv, chip):
        return remote(src.at[rows_of(chip, tok)], dst.at[x], send.at[chip], recv.at[x], at_chip(chip))

    def send_owned(own, src, landing, out, owners, send, landed, rsend, rrecv):
        def step(i, carry):
            chip = x - 1 - i
            at = rows_of(chip, tok)
            exchange_copy(src, landing, send, landed, chip).wait_recv()
            out[at, :] = (own[at, :] + landing[at, :].astype(jnp.float32)).astype(jnp.bfloat16)
            owner_copy(out, owners, rsend, rrecv, chip).start()
            return carry

        lax.fori_loop(0, x, step, 0)
        at = rows_of(x, tok)
        exchange_copy(src, landing, send, landed, x).wait_recv()
        own[at, :] = own[at, :] + landing[at, :].astype(jnp.float32)

    send_owned(av, sbv, rbv, gv, hv, ev_send, ev_recv, rv_send, rv_recv)

    @pl.when(late)
    def _():
        pl.semaphore_wait(ready, heads)
        lax.fori_loop(0, heads, send_up, 0)


    block_sums(dsb, qs, part_k)
    exchange(part_k, ak, sbk, rbk, ek_send, ek_recv)

    def query_step(i, carry):
        qb, tile = i // tiles, i % tiles
        grad = lax.dot_general(dsb[i], ks[qb], TN_DIMS, preferred_element_type=jnp.float32)
        grad = grad.astype(jnp.bfloat16)
        for h in range(TILE_HEADS):
            dq[rows_of(qb, BLK), rows_of(tile * TILE_HEADS + h, HD)] = grad[h * BLK:(h + 1) * BLK]
        return carry

    lax.fori_loop(0, blocks * tiles, query_step, 0)
    dq_copy = pltpu.make_async_copy(dq, dq_out.at[0], loc_sem.at[4])
    dq_copy.start()
    send_owned(ak, sbk, rbk, gk, hk, ek_send, ek_recv, rk_send, rk_recv)

    def owned_total(own, landing, recv, at):
        own_rows = own[rows_of(x, tok), :]

        def step(chip, total):
            block = landing.at[chip]
            remote(block, block, recv.at[chip], recv.at[chip], sibling).wait_recv()
            return total + landing[chip].astype(jnp.float32)

        dkv[at] = lax.fori_loop(x + 1, chips, step, own_rows).astype(jnp.bfloat16)

    owned_total(av, hv, rv_recv, 0)
    dv_copy = pltpu.make_async_copy(dkv.at[0], dv_out.at[0], loc_sem.at[5])
    dv_copy.start()
    owned_total(ak, hk, rk_recv, 1)
    dk_copy = pltpu.make_async_copy(dkv.at[1], dk_out.at[0], loc_sem.at[6])
    dk_copy.start()

    def left_gather(chip, carry):
        gather_copy(k, kbuf, k_send, k_recv, chip, at_chip(chip)).wait_send()
        gather_copy(v, vbuf, v_send, v_recv, chip, at_chip(chip)).wait_send()
        return carry

    def left_up(h, carry):
        up_copy(h).wait_send()
        return carry

    def left_lower(chip, carry):
        passed_on(kbuf, k_fwd, k_sib, chip).wait_send()
        passed_on(vbuf, v_fwd, v_sib, chip).wait_send()
        owner_copy(gv, hv, rv_send, rv_recv, chip).wait_send()
        owner_copy(gk, hk, rk_send, rk_recv, chip).wait_send()
        return carry

    def left_exchange(chip, carry):
        exchange_copy(sbv, rbv, ev_send, ev_recv, chip).wait_send()
        exchange_copy(sbk, rbk, ek_send, ek_recv, chip).wait_send()
        return carry

    lax.fori_loop(x, chips, left_gather, 0)
    lax.fori_loop(0, heads, left_up, 0)
    lax.fori_loop(0, x, left_lower, 0)
    lax.fori_loop(0, x + 1, left_exchange, 0)
    dq_copy.wait()
    dv_copy.wait()
    dk_copy.wait()


def hand_on(dq_in, dk_in, dv_in, dq_out, dk_out, dv_out, sems):
    pairs = ((dq_in, dq_out), (dk_in, dk_out), (dv_in, dv_out))
    copies = [pltpu.make_async_copy(a, b, sems.at[i]) for i, (a, b) in enumerate(pairs)]
    for copy in copies:
        copy.start()
    for copy in copies:
        copy.wait()


def per_device(pipes, ctxs, heads, queries, key_states, value_states, upstream, selected):
    tok = queries.shape[1]
    topb = selected.shape[3]
    blocks = tok // BLK
    chips = ctxs // 2
    tokens = tok * ctxs
    keys = topb * BLK
    tiles = GROUP // TILE_HEADS
    columns = TILE_HEADS * BLK
    width = GROUP * HD
    bf16, f32 = jnp.bfloat16, jnp.float32
    vmem = pltpu.VMEM
    dma = pltpu.SemaphoreType.DMA
    owned = (chips * tok, HD)
    scratch = [
        vmem((tokens // BLK, BLK, HD), bf16), vmem((tokens // BLK, BLK, HD), bf16),
        vmem((tok, width), bf16), vmem((tok, width), bf16),
        vmem((blocks * tiles, columns, HD), bf16), vmem((blocks * tiles, columns, HD), bf16),
        vmem((blocks, keys, HD), bf16),
        vmem((blocks * tiles, keys, columns), f32), vmem((blocks * tiles, keys, columns), bf16),
        vmem((blocks * tiles, keys, columns), bf16),
        vmem((blocks * (topb + 1), BLK, HD), f32), vmem((blocks * (topb + 1), BLK, HD), f32),
        vmem(owned, f32), vmem(owned, f32),
        vmem(owned, bf16), vmem(owned, bf16), vmem(owned, bf16), vmem(owned, bf16),
        vmem(owned, bf16), vmem(owned, bf16),
        vmem((chips, tok, HD), bf16), vmem((chips, tok, HD), bf16),
        vmem((tok, width), bf16), vmem((2, tok, HD), bf16),
        pltpu.SMEM((1, 1, blocks, topb), jnp.int32),
        pltpu.SMEM((blocks * ctxs * blocks,), jnp.int32),
        pltpu.SemaphoreType.REGULAR,
        dma((7,)), dma((heads,)), dma((heads,)),
    ] + [dma((chips,)) for _ in range(16)]
    sizes = (pipes, ctxs, heads, tok, topb)
    hbm = pl.BlockSpec(memory_space=pltpu.HBM)
    results = (
        jax.ShapeDtypeStruct(queries.shape, bf16),
        jax.ShapeDtypeStruct(key_states.shape, bf16),
        jax.ShapeDtypeStruct(value_states.shape, bf16),
    )
    grads = pl.pallas_call(
        functools.partial(body, sizes),
        out_shape=results,
        in_specs=[hbm] * 5,
        out_specs=(hbm, hbm, hbm),
        scratch_shapes=scratch,
        compiler_params=pltpu.CompilerParams(
            collective_id=0, has_side_effects=True, vmem_limit_bytes=60 * 1024 * 1024
        ),
        name="selected_attention_grads",
    )(
        selected,
        queries,
        key_states.reshape(blocks, BLK, HD),
        value_states.reshape(blocks, BLK, HD),
        upstream,
    )
    return pl.pallas_call(
        hand_on,
        out_shape=results,
        in_specs=[hbm] * 3,
        out_specs=(hbm, hbm, hbm),
        scratch_shapes=[dma((3,))],
        compiler_params=pltpu.CompilerParams(vmem_limit_bytes=60 * 1024 * 1024),
        name="hand_on_grads",
    )(*grads)


def solution(mesh):
    placed = (
        P("pipe", "ctx", "head"),
        P("pipe", "ctx", "head"),
        P("pipe", "ctx", "head"),
        P("pipe", ("ctx", "head"), None),
        P("pipe", "head", "ctx", None),
    )
    per = functools.partial(per_device, mesh.shape["pipe"], mesh.shape["ctx"], mesh.shape["head"])
    return jax.shard_map(
        per,
        mesh=mesh,
        in_specs=placed,
        out_specs=(P("pipe", "ctx", "head"), P("pipe", "ctx", "head"), P("pipe", "ctx", "head")),
        check_vma=False,
    )
```

```python
import functools

import jax
import jax.numpy as jnp
from jax import lax
from jax.experimental import pallas as pl
from jax.experimental.pallas import tpu as pltpu
from jax.sharding import PartitionSpec as P

HD = 128
BLK = 64
GROUP = 8
TILE_HEADS = 4
SCALE = HD ** (-0.5)
LOG2E = 1.4426950408889634

NT_DIMS = (((1,), (1,)), ((), ()))
TN_DIMS = (((0,), (0,)), ((), ()))


def rows_of(index, size):
    return pl.ds(pl.multiple_of(index * size, size), size)


def body(sizes, sel_in, q, k, v, up, dq_out, dk_out, dv_out, *scratch):
    pipes, ctxs, heads, tok, topb = sizes
    (
        kbuf, vbuf, qv, og, qs, os, ks, pf, pb, dsb, part_v, part_k,
        av, ak, sbv, sbk, rbv, rbk, gv, gk, hv, hk, dq, dkv, sel, tbl, ready,
        loc_sem, up_send, up_recv,
        k_send, k_recv, k_fwd, k_sib, v_send, v_recv, v_fwd, v_sib,
        ev_send, ev_recv, ek_send, ek_recv,
        rv_send, rv_recv, rk_send, rk_recv,
    ) = scratch
    chips = ctxs // 2
    blocks = tok // BLK
    all_blocks = ctxs * blocks
    slots = topb + 1
    tiles = GROUP // TILE_HEADS
    width = GROUP * HD
    keys = topb * BLK
    up_rows = tok // heads

    z = lax.axis_index("pipe")
    c = lax.axis_index("ctx")
    y = lax.axis_index("head")
    x = c // 2
    core = c % 2
    other = c + 1 - 2 * core
    z_prev = (z + pipes - 1) % pipes
    z_next = (z + 1) % pipes

    def blocks_of(owner):
        return pl.ds(owner * blocks, blocks)

    def at_chip(chip):
        return (z, chip * 2 + core, y)

    sibling = (z, other, y)
    near_first = sorted(range(1, chips), key=lambda d: min(d, chips - d))

    def later_chips(step):
        for d in reversed(near_first):
            @pl.when(x + d < chips)
            def _(d=d):
                step(x + d)

    def earlier_chips(step, order):
        for d in order:
            @pl.when(x >= d)
            def _(d=d):
                step(x - d)


    def remote(src, dst, send, recv, target):
        return pltpu.make_async_remote_copy(
            src_ref=src, dst_ref=dst, send_sem=send, recv_sem=recv,
            device_id=target, device_id_type=pl.DeviceIdType.MESH,
        )

    q_copy = pltpu.make_async_copy(q.at[0], qv, loc_sem.at[0])
    k_copy = pltpu.make_async_copy(k, kbuf.at[blocks_of(c)], loc_sem.at[1])
    v_copy = pltpu.make_async_copy(v, vbuf.at[blocks_of(c)], loc_sem.at[2])
    sel_copy = pltpu.make_async_copy(sel_in, sel, loc_sem.at[3])
    sel_copy.start()
    q_copy.start()
    k_copy.start()
    v_copy.start()

    barrier = pltpu.get_barrier_semaphore()

    def told_later(section):
        return jnp.logical_or(section == 0, jnp.logical_and(section == 1, c == 0))

    def as_int(flag):
        return jnp.where(flag, jnp.int32(1), jnp.int32(0))

    late = told_later(z)
    next_late = told_later(z_next)

    def greet(semaphore, target):
        pl.semaphore_signal(semaphore, inc=1, device_id=target, device_id_type=pl.DeviceIdType.MESH)

    def greet_chip(chip, carry):
        greet(barrier, at_chip(chip))
        return carry

    def greet_receiver(h, carry):
        greet(barrier, (z_prev, c, h))
        return carry

    def greet_sender(h, carry):
        greet(barrier, (z_next, c, h))
        return carry

    def tell_sender(h, carry):
        greet(ready, (z_next, c, h))
        return carry

    lax.fori_loop(0, x, greet_chip, 0)

    @pl.when(core == 1)
    def _():
        greet(barrier, sibling)

    @pl.when(jnp.logical_not(next_late))
    def _():
        lax.fori_loop(0, heads, greet_sender, 0)

    @pl.when(late)
    def _():
        lax.fori_loop(0, heads, greet_receiver, 0)

    expected = chips - 1 - x + (1 - core) + heads * (1 - as_int(late)) + heads * as_int(next_late)

    @pl.when(expected > 0)
    def _():
        pl.semaphore_wait(barrier, expected)

    def gather_copy(src, buf, send, recv, chip, target):
        return remote(src, buf.at[blocks_of(c)], send.at[chip], recv.at[x], target)

    def send_keys(chip):
        gather_copy(k, kbuf, k_send, k_recv, chip, at_chip(chip)).start()

    def send_values(chip):
        gather_copy(v, vbuf, v_send, v_recv, chip, at_chip(chip)).start()

    def send_to_sibling():
        gather_copy(k, kbuf, k_send, k_sib, x, sibling).start()
        gather_copy(v, vbuf, v_send, v_sib, x, sibling).start()

    def up_copy(h):
        return remote(
            up.at[0, :, rows_of(h, width)], og.at[rows_of(y, up_rows)],
            up_send.at[h], up_recv.at[y], (z_prev, c, h),
        )

    def send_up(h, carry):
        up_copy(h).start()
        return carry

    later_chips(send_keys)

    @pl.when(core == 0)
    def _():
        send_to_sibling()

    @pl.when(next_late)
    def _():
        lax.fori_loop(0, heads, tell_sender, 0)

    @pl.when(jnp.logical_not(late))
    def _():
        lax.fori_loop(0, heads, send_up, 0)

    sel_copy.wait()

    def slot_row(j, carry):
        for qb in range(blocks):
            slot = jnp.int32(topb)
            for t in range(topb):
                slot = jnp.where(sel[0, 0, qb, t] == j, jnp.int32(t), slot)
            tbl[qb * all_blocks + j] = slot + qb * slots
        return carry

    lax.fori_loop(0, all_blocks, slot_row, 0)
    zero_rows = jnp.zeros((BLK, HD), jnp.float32)
    for qb in range(blocks):
        part_v[qb * slots + topb] = zero_rows
        part_k[qb * slots + topb] = zero_rows

    def passed_on(buf, fwd, sib, chip):
        block = buf.at[blocks_of(chip * 2 + core)]
        return remote(block, block, fwd.at[chip], sib.at[chip], sibling)

    def arrived(buf, recv, chip):
        block = buf.at[blocks_of(chip * 2 + core)]
        return remote(block, block, recv.at[chip], recv.at[chip], sibling)

    def from_sibling(buf, sib, chip):
        block = buf.at[blocks_of(chip * 2 + 1 - core)]
        return remote(block, block, sib.at[chip], sib.at[chip], sibling)

    def forward_all(buf, recv, fwd, sib):
        def step(chip):
            arrived(buf, recv, chip).wait_recv()
            passed_on(buf, fwd, sib, chip).start()

        earlier_chips(step, near_first)

    def wait_sibling(buf, sib, count):
        def step(chip, carry):
            from_sibling(buf, sib, chip).wait_recv()
            return carry

        lax.fori_loop(0, count, step, 0)

    def keys_left(chip, carry):
        gather_copy(k, kbuf, k_send, k_recv, chip, at_chip(chip)).wait_send()
        return carry

    lax.fori_loop(x + 1, chips, keys_left, 0)
    later_chips(send_values)

    @pl.when(core == 1)
    def _():
        from_sibling(kbuf, k_sib, x).wait_recv()
        send_to_sibling()

    forward_all(kbuf, k_recv, k_fwd, k_sib)
    q_copy.wait()
    k_copy.wait()
    v_copy.wait()
    wait_sibling(kbuf, k_sib, x + 1 - core)

    def chosen_rows(buf, qb):
        mine = c * blocks + qb
        return jnp.concatenate(
            [buf[jnp.minimum(sel[0, 0, qb, t], mine)] for t in range(topb)], axis=0
        )

    def head_rows(ref, qb, tile):
        return jnp.concatenate(
            [ref[rows_of(qb, BLK), rows_of(tile * TILE_HEADS + h, HD)] for h in range(TILE_HEADS)],
            axis=0,
        )

    columns = TILE_HEADS * BLK

    def score_step(i, carry):
        qb, tile = i // tiles, i % tiles
        mine = c * blocks + qb
        key_rows = chosen_rows(kbuf, qb)
        ks[qb] = key_rows
        query_rows = head_rows(qv, qb, tile)
        qs[i] = query_rows
        scores = lax.dot_general(key_rows, query_rows, NT_DIMS, preferred_element_type=jnp.float32)
        key_at = lax.broadcasted_iota(jnp.int32, (BLK, columns), 0)
        query_at = lax.broadcasted_iota(jnp.int32, (BLK, columns), 1) % BLK
        pieces = [jnp.where(key_at <= query_at, scores[:BLK], -jnp.inf)]
        for t in range(1, topb):
            shift = jnp.where(sel[0, 0, qb, t] > mine, jnp.float32(-jnp.inf), jnp.float32(0.0))
            pieces.append(scores[t * BLK:(t + 1) * BLK] + shift)
        scores = jnp.concatenate(pieces, axis=0)
        top = jnp.max(scores, axis=0, keepdims=True)
        weights = jnp.exp2((scores - top) * (SCALE * LOG2E))
        weights = weights * (1.0 / jnp.sum(weights, axis=0, keepdims=True))
        pf[i] = weights
        pb[i] = weights.astype(jnp.bfloat16)
        return carry

    lax.fori_loop(0, blocks * tiles, score_step, 0)

    def up_arrived(h, carry):
        block = og.at[rows_of(h, up_rows)]
        remote(block, block, up_recv.at[h], up_recv.at[h], sibling).wait_recv()
        return carry

    lax.fori_loop(0, heads, up_arrived, 0)

    def block_sums(lhs, rhs, part):
        def step(qb, carry):
            total = jnp.dot(lhs[qb * tiles], rhs[qb * tiles], preferred_element_type=jnp.float32)
            for tile in range(1, tiles):
                total += jnp.dot(
                    lhs[qb * tiles + tile], rhs[qb * tiles + tile], preferred_element_type=jnp.float32
                )
            for t in range(topb):
                part[qb * slots + t] = total[t * BLK:(t + 1) * BLK]
            return carry

        lax.fori_loop(0, blocks, step, 0)

    def grad_rows(i, carry):
        os[i] = head_rows(og, i // tiles, i % tiles)
        return carry

    lax.fori_loop(0, blocks * tiles, grad_rows, 0)
    block_sums(pb, os, part_v)

    def exchange_copy(src, dst, send, recv, chip):
        return remote(
            src.at[rows_of(chip, tok)], dst.at[rows_of(chip, tok)], send.at[chip], recv.at[chip], sibling
        )

    def exchange(part, own, out, landing, send, recv):
        def owner_block(owner, b):
            j = owner * blocks + b
            total = part[tbl[j]]
            for qb in range(1, blocks):
                total = total + part[tbl[qb * all_blocks + j]]
            return total

        def step(chip, carry):
            for b in range(blocks):
                at = rows_of(chip * blocks + b, BLK)
                out[at, :] = owner_block(chip * 2 + 1 - core, b).astype(jnp.bfloat16)
            exchange_copy(out, landing, send, recv, chip).start()
            for b in range(blocks):
                at = rows_of(chip * blocks + b, BLK)
                own[at, :] = owner_block(chip * 2 + core, b)
            return carry

        lax.fori_loop(0, x + 1, step, 0)

    exchange(part_v, av, sbv, rbv, ev_send, ev_recv)

    def score_grad_step(i, carry):
        qb = i // tiles
        value_rows = chosen_rows(vbuf, qb)
        weight_grad = lax.dot_general(value_rows, os[i], NT_DIMS, preferred_element_type=jnp.float32)
        weights = pf[i]
        delta = jnp.sum(weights * weight_grad, axis=0, keepdims=True)
        dsb[i] = (weights * (weight_grad - delta) * SCALE).astype(jnp.bfloat16)
        return carry


    def owner_copy(src, dst, send, recv, chip):
        return remote(src.at[rows_of(chip, tok)], dst.at[x], send.at[chip], recv.at[x], at_chip(chip))

    def send_owned(own, src, landing, out, owners, send, landed, rsend, rrecv):
        def step(chip):
            at = rows_of(chip, tok)
            exchange_copy(src, landing, send, landed, chip).wait_recv()
            out[at, :] = (own[at, :] + landing[at, :].astype(jnp.float32)).astype(jnp.bfloat16)
            owner_copy(out, owners, rsend, rrecv, chip).start()

        earlier_chips(step, near_first[::-1])
        at = rows_of(x, tok)
        exchange_copy(src, landing, send, landed, x).wait_recv()
        own[at, :] = own[at, :] + landing[at, :].astype(jnp.float32)

    send_owned(av, sbv, rbv, gv, hv, ev_send, ev_recv, rv_send, rv_recv)
    forward_all(vbuf, v_recv, v_fwd, v_sib)

    @pl.when(late)
    def _():
        pl.semaphore_wait(ready, heads)
        lax.fori_loop(0, heads, send_up, 0)


    wait_sibling(vbuf, v_sib, x + 1)
    lax.fori_loop(0, blocks * tiles, score_grad_step, 0)
    block_sums(dsb, qs, part_k)
    exchange(part_k, ak, sbk, rbk, ek_send, ek_recv)

    def query_step(i, carry):
        qb, tile = i // tiles, i % tiles
        grad = lax.dot_general(dsb[i], ks[qb], TN_DIMS, preferred_element_type=jnp.float32)
        grad = grad.astype(jnp.bfloat16)
        for h in range(TILE_HEADS):
            dq[rows_of(qb, BLK), rows_of(tile * TILE_HEADS + h, HD)] = grad[h * BLK:(h + 1) * BLK]
        return carry

    lax.fori_loop(0, blocks * tiles, query_step, 0)
    dq_copy = pltpu.make_async_copy(dq, dq_out.at[0], loc_sem.at[4])
    dq_copy.start()
    send_owned(ak, sbk, rbk, gk, hk, ek_send, ek_recv, rk_send, rk_recv)

    def owned_total(own, landing, recv, at):
        own_rows = own[rows_of(x, tok), :]

        def step(chip, total):
            block = landing.at[chip]
            remote(block, block, recv.at[chip], recv.at[chip], sibling).wait_recv()
            return total + landing[chip].astype(jnp.float32)

        dkv[at] = lax.fori_loop(x + 1, chips, step, own_rows).astype(jnp.bfloat16)

    owned_total(av, hv, rv_recv, 0)
    dv_copy = pltpu.make_async_copy(dkv.at[0], dv_out.at[0], loc_sem.at[5])
    dv_copy.start()
    owned_total(ak, hk, rk_recv, 1)
    dk_copy = pltpu.make_async_copy(dkv.at[1], dk_out.at[0], loc_sem.at[6])
    dk_copy.start()

    def left_gather(chip, carry):
        @pl.when(chip == x)
        def _():
            gather_copy(k, kbuf, k_send, k_recv, chip, at_chip(chip)).wait_send()

        gather_copy(v, vbuf, v_send, v_recv, chip, at_chip(chip)).wait_send()
        return carry

    def left_up(h, carry):
        up_copy(h).wait_send()
        return carry

    def left_lower(chip, carry):
        passed_on(kbuf, k_fwd, k_sib, chip).wait_send()
        passed_on(vbuf, v_fwd, v_sib, chip).wait_send()
        owner_copy(gv, hv, rv_send, rv_recv, chip).wait_send()
        owner_copy(gk, hk, rk_send, rk_recv, chip).wait_send()
        return carry

    def left_exchange(chip, carry):
        exchange_copy(sbv, rbv, ev_send, ev_recv, chip).wait_send()
        exchange_copy(sbk, rbk, ek_send, ek_recv, chip).wait_send()
        return carry

    lax.fori_loop(x, chips, left_gather, 0)
    lax.fori_loop(0, heads, left_up, 0)
    lax.fori_loop(0, x, left_lower, 0)
    lax.fori_loop(0, x + 1, left_exchange, 0)
    dq_copy.wait()
    dv_copy.wait()
    dk_copy.wait()


def hand_on(dq_in, dk_in, dv_in, dq_out, dk_out, dv_out):
    dq_out[...] = dq_in[...]
    dk_out[...] = dk_in[...]
    dv_out[...] = dv_in[...]


def per_device(pipes, ctxs, heads, queries, key_states, value_states, upstream, selected):
    tok = queries.shape[1]
    topb = selected.shape[3]
    blocks = tok // BLK
    chips = ctxs // 2
    tokens = tok * ctxs
    keys = topb * BLK
    tiles = GROUP // TILE_HEADS
    columns = TILE_HEADS * BLK
    width = GROUP * HD
    bf16, f32 = jnp.bfloat16, jnp.float32
    vmem = pltpu.VMEM
    dma = pltpu.SemaphoreType.DMA
    owned = (chips * tok, HD)
    scratch = [
        vmem((tokens // BLK, BLK, HD), bf16), vmem((tokens // BLK, BLK, HD), bf16),
        vmem((tok, width), bf16), vmem((tok, width), bf16),
        vmem((blocks * tiles, columns, HD), bf16), vmem((blocks * tiles, columns, HD), bf16),
        vmem((blocks, keys, HD), bf16),
        vmem((blocks * tiles, keys, columns), f32), vmem((blocks * tiles, keys, columns), bf16),
        vmem((blocks * tiles, keys, columns), bf16),
        vmem((blocks * (topb + 1), BLK, HD), f32), vmem((blocks * (topb + 1), BLK, HD), f32),
        vmem(owned, f32), vmem(owned, f32),
        vmem(owned, bf16), vmem(owned, bf16), vmem(owned, bf16), vmem(owned, bf16),
        vmem(owned, bf16), vmem(owned, bf16),
        vmem((chips, tok, HD), bf16), vmem((chips, tok, HD), bf16),
        vmem((tok, width), bf16), vmem((2, tok, HD), bf16),
        pltpu.SMEM((1, 1, blocks, topb), jnp.int32),
        pltpu.SMEM((blocks * ctxs * blocks,), jnp.int32),
        pltpu.SemaphoreType.REGULAR,
        dma((7,)), dma((heads,)), dma((heads,)),
    ] + [dma((chips,)) for _ in range(16)]
    sizes = (pipes, ctxs, heads, tok, topb)
    hbm = pl.BlockSpec(memory_space=pltpu.HBM)
    results = (
        jax.ShapeDtypeStruct(queries.shape, bf16),
        jax.ShapeDtypeStruct(key_states.shape, bf16),
        jax.ShapeDtypeStruct(value_states.shape, bf16),
    )
    grads = pl.pallas_call(
        functools.partial(body, sizes),
        out_shape=results,
        in_specs=[hbm] * 5,
        out_specs=(hbm, hbm, hbm),
        scratch_shapes=scratch,
        compiler_params=pltpu.CompilerParams(
            collective_id=0, has_side_effects=True, vmem_limit_bytes=60 * 1024 * 1024
        ),
        name="selected_attention_grads",
    )(
        selected,
        queries,
        key_states.reshape(blocks, BLK, HD),
        value_states.reshape(blocks, BLK, HD),
        upstream,
    )
    whole = pl.BlockSpec(memory_space=pltpu.VMEM)
    return pl.pallas_call(
        hand_on,
        out_shape=results,
        in_specs=[whole] * 3,
        out_specs=(whole, whole, whole),
        name="hand_on_grads",
    )(*grads)


def solution(mesh):
    placed = (
        P("pipe", "ctx", "head"),
        P("pipe", "ctx", "head"),
        P("pipe", "ctx", "head"),
        P("pipe", ("ctx", "head"), None),
        P("pipe", "head", "ctx", None),
    )
    per = functools.partial(per_device, mesh.shape["pipe"], mesh.shape["ctx"], mesh.shape["head"])
    return jax.shard_map(
        per,
        mesh=mesh,
        in_specs=placed,
        out_specs=(P("pipe", "ctx", "head"), P("pipe", "ctx", "head"), P("pipe", "ctx", "head")),
        check_vma=False,
    )
```

```python
import functools

import jax
import jax.numpy as jnp
from jax import lax
from jax.experimental import pallas as pl
from jax.experimental.pallas import tpu as pltpu
from jax.sharding import PartitionSpec as P

HD = 128
BLK = 64
GROUP = 8
TILE_HEADS = 4
SCALE = HD ** (-0.5)
LOG2E = 1.4426950408889634

NT_DIMS = (((1,), (1,)), ((), ()))
TN_DIMS = (((0,), (0,)), ((), ()))


def rows_of(index, size):
    return pl.ds(pl.multiple_of(index * size, size), size)


def body(sizes, sel_in, q, k, v, up, dq_out, dk_out, dv_out, *scratch):
    pipes, ctxs, heads, tok, topb = sizes
    (
        kbuf, vbuf, qv, og, qs, os, ks, pf, pb, dsb, part_v, part_k,
        av, ak, sbv, sbk, rbv, rbk, gv, gk, hv, hk, dq, dkv, sel, tbl, ready,
        loc_sem, up_send, up_recv,
        k_send, k_recv, k_fwd, k_sib, v_send, v_recv, v_fwd, v_sib,
        ev_send, ev_recv, ek_send, ek_recv,
        rv_send, rv_recv, rk_send, rk_recv,
    ) = scratch
    chips = ctxs // 2
    blocks = tok // BLK
    all_blocks = ctxs * blocks
    slots = topb + 1
    tiles = GROUP // TILE_HEADS
    width = GROUP * HD
    keys = topb * BLK
    up_rows = tok // heads

    z = lax.axis_index("pipe")
    c = lax.axis_index("ctx")
    y = lax.axis_index("head")
    x = c // 2
    core = c % 2
    other = c + 1 - 2 * core
    z_prev = (z + pipes - 1) % pipes
    z_next = (z + 1) % pipes

    def blocks_of(owner):
        return pl.ds(owner * blocks, blocks)

    def at_chip(chip):
        return (z, chip * 2 + core, y)

    sibling = (z, other, y)
    near_first = sorted(range(1, chips), key=lambda d: min(d, chips - d))

    def later_chips(step):
        for d in reversed(near_first):
            @pl.when(x + d < chips)
            def _(d=d):
                step(x + d)

    def earlier_chips(step, order):
        for d in order:
            @pl.when(x > d)
            def _(d=d):
                step(x - d)

        @pl.when(x > 0)
        def _():
            step(0)


    def remote(src, dst, send, recv, target):
        return pltpu.make_async_remote_copy(
            src_ref=src, dst_ref=dst, send_sem=send, recv_sem=recv,
            device_id=target, device_id_type=pl.DeviceIdType.MESH,
        )

    q_copy = pltpu.make_async_copy(q.at[0], qv, loc_sem.at[0])
    k_copy = pltpu.make_async_copy(k, kbuf.at[blocks_of(c)], loc_sem.at[1])
    v_copy = pltpu.make_async_copy(v, vbuf.at[blocks_of(c)], loc_sem.at[2])
    sel_copy = pltpu.make_async_copy(sel_in, sel, loc_sem.at[3])
    sel_copy.start()
    q_copy.start()
    k_copy.start()
    v_copy.start()

    barrier = pltpu.get_barrier_semaphore()

    def told_later(section):
        return jnp.logical_or(section == 0, jnp.logical_and(section == 1, c == 0))

    def as_int(flag):
        return jnp.where(flag, jnp.int32(1), jnp.int32(0))

    late = told_later(z)
    next_late = told_later(z_next)

    def greet(semaphore, target):
        pl.semaphore_signal(semaphore, inc=1, device_id=target, device_id_type=pl.DeviceIdType.MESH)

    def greet_chip(chip, carry):
        greet(barrier, at_chip(chip))
        return carry

    def greet_receiver(h, carry):
        greet(barrier, (z_prev, c, h))
        return carry

    def greet_sender(h, carry):
        greet(barrier, (z_next, c, h))
        return carry

    def tell_sender(h, carry):
        greet(ready, (z_next, c, h))
        return carry

    lax.fori_loop(0, x, greet_chip, 0)

    @pl.when(core == 1)
    def _():
        greet(barrier, sibling)

    @pl.when(jnp.logical_not(next_late))
    def _():
        lax.fori_loop(0, heads, greet_sender, 0)

    @pl.when(late)
    def _():
        lax.fori_loop(0, heads, greet_receiver, 0)

    expected = chips - 1 - x + (1 - core) + heads * (1 - as_int(late)) + heads * as_int(next_late)

    @pl.when(expected > 0)
    def _():
        pl.semaphore_wait(barrier, expected)

    def gather_copy(src, buf, send, recv, chip, target):
        return remote(src, buf.at[blocks_of(c)], send.at[chip], recv.at[x], target)

    def send_keys(chip):
        gather_copy(k, kbuf, k_send, k_recv, chip, at_chip(chip)).start()

    def send_values(chip):
        gather_copy(v, vbuf, v_send, v_recv, chip, at_chip(chip)).start()

    def send_to_sibling():
        gather_copy(k, kbuf, k_send, k_sib, x, sibling).start()
        gather_copy(v, vbuf, v_send, v_sib, x, sibling).start()

    def up_copy(h):
        return remote(
            up.at[0, :, rows_of(h, width)], og.at[rows_of(y, up_rows)],
            up_send, up_recv, (z_prev, c, h),
        )

    def send_up(h, carry):
        up_copy(h).start()
        return carry

    later_chips(send_keys)

    @pl.when(core == 0)
    def _():
        send_to_sibling()

    @pl.when(next_late)
    def _():
        lax.fori_loop(0, heads, tell_sender, 0)

    @pl.when(jnp.logical_not(late))
    def _():
        lax.fori_loop(0, heads, send_up, 0)

    sel_copy.wait()

    def slot_row(j, carry):
        for qb in range(blocks):
            slot = jnp.int32(topb)
            for t in range(topb):
                slot = jnp.where(sel[0, 0, qb, t] == j, jnp.int32(t), slot)
            tbl[qb * all_blocks + j] = slot + qb * slots
        return carry

    lax.fori_loop(0, all_blocks, slot_row, 0)
    zero_rows = jnp.zeros((BLK, HD), jnp.float32)
    for qb in range(blocks):
        part_v[qb * slots + topb] = zero_rows
        part_k[qb * slots + topb] = zero_rows

    def passed_on(buf, fwd, sib, chip):
        block = buf.at[blocks_of(chip * 2 + core)]
        return remote(block, block, fwd.at[chip], sib.at[chip], sibling)

    def arrived(buf, recv, chip):
        block = buf.at[blocks_of(chip * 2 + core)]
        return remote(block, block, recv.at[chip], recv.at[chip], sibling)

    def from_sibling(buf, sib, chip):
        block = buf.at[blocks_of(chip * 2 + 1 - core)]
        return remote(block, block, sib.at[chip], sib.at[chip], sibling)

    def forward_all(buf, recv, fwd, sib):
        def step(chip):
            arrived(buf, recv, chip).wait_recv()
            passed_on(buf, fwd, sib, chip).start()

        earlier_chips(step, near_first)

    def wait_sibling(buf, sib, count):
        def step(chip, carry):
            from_sibling(buf, sib, chip).wait_recv()
            return carry

        lax.fori_loop(0, count, step, 0)

    def key_left(chip):
        gather_copy(k, kbuf, k_send, k_recv, chip, at_chip(chip)).wait_send()

    @pl.when(x > 0)
    def _():
        later_chips(key_left)

    later_chips(send_values)

    @pl.when(core == 1)
    def _():
        from_sibling(kbuf, k_sib, x).wait_recv()
        send_to_sibling()

    forward_all(kbuf, k_recv, k_fwd, k_sib)
    q_copy.wait()
    k_copy.wait()
    v_copy.wait()
    wait_sibling(kbuf, k_sib, x + 1 - core)

    def chosen_rows(buf, qb):
        mine = c * blocks + qb
        return jnp.concatenate(
            [buf[jnp.minimum(sel[0, 0, qb, t], mine)] for t in range(topb)], axis=0
        )

    def head_rows(ref, qb, tile):
        return jnp.concatenate(
            [ref[rows_of(qb, BLK), rows_of(tile * TILE_HEADS + h, HD)] for h in range(TILE_HEADS)],
            axis=0,
        )

    columns = TILE_HEADS * BLK

    def score_step(i, carry):
        qb, tile = i // tiles, i % tiles
        mine = c * blocks + qb
        key_rows = chosen_rows(kbuf, qb)
        ks[qb] = key_rows
        query_rows = head_rows(qv, qb, tile)
        qs[i] = query_rows
        scores = lax.dot_general(key_rows, query_rows, NT_DIMS, preferred_element_type=jnp.float32)
        key_at = lax.broadcasted_iota(jnp.int32, (BLK, columns), 0)
        query_at = lax.broadcasted_iota(jnp.int32, (BLK, columns), 1) % BLK
        pieces = [jnp.where(key_at <= query_at, scores[:BLK], -jnp.inf)]
        for t in range(1, topb):
            shift = jnp.where(sel[0, 0, qb, t] > mine, jnp.float32(-jnp.inf), jnp.float32(0.0))
            pieces.append(scores[t * BLK:(t + 1) * BLK] + shift)
        scores = jnp.concatenate(pieces, axis=0)
        top = jnp.max(scores, axis=0, keepdims=True)
        weights = jnp.exp2((scores - top) * (SCALE * LOG2E))
        weights = weights * (1.0 / jnp.sum(weights, axis=0, keepdims=True))
        pf[i] = weights
        pb[i] = weights.astype(jnp.bfloat16)
        return carry

    lax.fori_loop(0, blocks * tiles, score_step, 0, unroll=True)

    all_up = remote(og, og, up_send, up_recv, sibling)
    all_up.wait_recv()

    def block_sums(lhs, rhs, part):
        def step(qb, carry):
            total = jnp.dot(lhs[qb * tiles], rhs[qb * tiles], preferred_element_type=jnp.float32)
            for tile in range(1, tiles):
                total += jnp.dot(
                    lhs[qb * tiles + tile], rhs[qb * tiles + tile], preferred_element_type=jnp.float32
                )
            for t in range(topb):
                part[qb * slots + t] = total[t * BLK:(t + 1) * BLK]
            return carry

        lax.fori_loop(0, blocks, step, 0, unroll=True)

    def grad_rows(i, carry):
        os[i] = head_rows(og, i // tiles, i % tiles)
        return carry

    lax.fori_loop(0, blocks * tiles, grad_rows, 0, unroll=True)
    block_sums(pb, os, part_v)

    half = chips // 2

    def farthest_first(count, step):
        def turn(i, carry):
            d = half + (1 - 2 * (i % 2)) * ((i + 1) // 2)

            @pl.when(x >= d)
            def _():
                step(x - d)

            return carry

        lax.fori_loop(0, count, turn, 0)

    def exchange_copy(src, dst, send, recv, chip):
        at = rows_of(chip, tok)
        return remote(src.at[at], dst.at[at], send.at[chip], recv.at[chip], sibling)

    def exchange(part, own, out, landing, send, recv):
        def owner_block(owner, b):
            j = owner * blocks + b
            total = part[tbl[j]]
            for qb in range(1, blocks):
                total = total + part[tbl[qb * all_blocks + j]]
            return total

        def step(chip):
            for b in range(blocks):
                at = rows_of(chip * blocks + b, BLK)
                out[at, :] = owner_block(chip * 2 + 1 - core, b).astype(jnp.bfloat16)
            exchange_copy(out, landing, send, recv, chip).start()
            for b in range(blocks):
                own[rows_of(chip * blocks + b, BLK), :] = owner_block(chip * 2 + core, b)

        farthest_first(chips, step)

    exchange(part_v, av, sbv, rbv, ev_send, ev_recv)

    def score_grad_step(i, carry):
        qb = i // tiles
        value_rows = chosen_rows(vbuf, qb)
        weight_grad = lax.dot_general(value_rows, os[i], NT_DIMS, preferred_element_type=jnp.float32)
        weights = pf[i]
        delta = jnp.sum(weights * weight_grad, axis=0, keepdims=True)
        dsb[i] = (weights * (weight_grad - delta) * SCALE).astype(jnp.bfloat16)
        return carry


    def owner_copy(src, dst, send, recv, chip):
        return remote(src.at[rows_of(chip, tok)], dst.at[x], send.at[chip], recv.at[x], at_chip(chip))

    def send_owned(own, src, landing, out, owners, send, landed, rsend, rrecv):
        def step(chip):
            at = rows_of(chip, tok)
            exchange_copy(src, landing, send, landed, chip).wait_recv()
            out[at, :] = (own[at, :] + landing[at, :].astype(jnp.float32)).astype(jnp.bfloat16)
            owner_copy(out, owners, rsend, rrecv, chip).start()

        farthest_first(chips - 1, step)
        at = rows_of(x, tok)
        exchange_copy(src, landing, send, landed, x).wait_recv()
        own[at, :] = own[at, :] + landing[at, :].astype(jnp.float32)

    send_owned(av, sbv, rbv, gv, hv, ev_send, ev_recv, rv_send, rv_recv)
    forward_all(vbuf, v_recv, v_fwd, v_sib)

    @pl.when(late)
    def _():
        pl.semaphore_wait(ready, heads)
        lax.fori_loop(0, heads, send_up, 0)


    wait_sibling(vbuf, v_sib, x + 1)
    lax.fori_loop(0, blocks * tiles, score_grad_step, 0, unroll=True)
    block_sums(dsb, qs, part_k)
    exchange(part_k, ak, sbk, rbk, ek_send, ek_recv)

    def query_step(i, carry):
        qb, tile = i // tiles, i % tiles
        grad = lax.dot_general(dsb[i], ks[qb], TN_DIMS, preferred_element_type=jnp.float32)
        grad = grad.astype(jnp.bfloat16)
        for h in range(TILE_HEADS):
            dq[rows_of(qb, BLK), rows_of(tile * TILE_HEADS + h, HD)] = grad[h * BLK:(h + 1) * BLK]
        return carry

    lax.fori_loop(0, blocks * tiles, query_step, 0, unroll=True)
    dq_copy = pltpu.make_async_copy(dq, dq_out.at[0], loc_sem.at[4])
    dq_copy.start()
    send_owned(ak, sbk, rbk, gk, hk, ek_send, ek_recv, rk_send, rk_recv)

    def left_gather(chip, carry):
        @pl.when(jnp.logical_or(chip == x, x == 0))
        def _():
            gather_copy(k, kbuf, k_send, k_recv, chip, at_chip(chip)).wait_send()

        gather_copy(v, vbuf, v_send, v_recv, chip, at_chip(chip)).wait_send()
        return carry

    def left_lower(chip, carry):
        passed_on(kbuf, k_fwd, k_sib, chip).wait_send()
        passed_on(vbuf, v_fwd, v_sib, chip).wait_send()
        owner_copy(gv, hv, rv_send, rv_recv, chip).wait_send()
        return carry

    def left_exchange(chip, carry):
        exchange_copy(sbv, rbv, ev_send, ev_recv, chip).wait_send()
        exchange_copy(sbk, rbk, ek_send, ek_recv, chip).wait_send()
        return carry

    lax.fori_loop(x, chips, left_gather, 0)
    all_up.wait_send()
    lax.fori_loop(0, x, left_lower, 0)
    lax.fori_loop(0, x + 1, left_exchange, 0)
    def owned_total(own, landing, recv, at):
        own_rows = own[rows_of(x, tok), :]

        def step(chip, total):
            block = landing.at[chip]
            remote(block, block, recv.at[chip], recv.at[chip], sibling).wait_recv()
            return total + landing[chip].astype(jnp.float32)

        dkv[at] = lax.fori_loop(x + 1, chips, step, own_rows).astype(jnp.bfloat16)

    owned_total(av, hv, rv_recv, 0)
    dv_copy = pltpu.make_async_copy(dkv.at[0], dv_out.at[0], loc_sem.at[5])
    dv_copy.start()
    owned_total(ak, hk, rk_recv, 1)
    dk_copy = pltpu.make_async_copy(dkv.at[1], dk_out.at[0], loc_sem.at[6])
    dk_copy.start()

    def left_owner_keys(chip, carry):
        owner_copy(gk, hk, rk_send, rk_recv, chip).wait_send()
        return carry

    lax.fori_loop(0, x, left_owner_keys, 0)
    dq_copy.wait()
    dv_copy.wait()
    dk_copy.wait()


def hand_on(dq_in, dk_in, dv_in, dq_out, dk_out, dv_out, dq, dk, dv, in_sems, out_sems):
    held = (dq, dk, dv)
    arriving = [
        pltpu.make_async_copy(a, b, in_sems.at[i])
        for i, (a, b) in enumerate(zip((dq_in, dk_in, dv_in), held))
    ]
    leaving = [
        pltpu.make_async_copy(a, b, out_sems.at[i])
        for i, (a, b) in enumerate(zip(held, (dq_out, dk_out, dv_out)))
    ]
    for copy in arriving:
        copy.start()
    for there, back in zip(arriving, leaving):
        there.wait()
        back.start()
    for copy in leaving:
        copy.wait()


def per_device(pipes, ctxs, heads, queries, key_states, value_states, upstream, selected):
    tok = queries.shape[1]
    topb = selected.shape[3]
    blocks = tok // BLK
    chips = ctxs // 2
    tokens = tok * ctxs
    keys = topb * BLK
    tiles = GROUP // TILE_HEADS
    columns = TILE_HEADS * BLK
    width = GROUP * HD
    bf16, f32 = jnp.bfloat16, jnp.float32
    vmem = pltpu.VMEM
    dma = pltpu.SemaphoreType.DMA
    owned = (chips * tok, HD)
    scratch = [
        vmem((tokens // BLK, BLK, HD), bf16), vmem((tokens // BLK, BLK, HD), bf16),
        vmem((tok, width), bf16), vmem((tok, width), bf16),
        vmem((blocks * tiles, columns, HD), bf16), vmem((blocks * tiles, columns, HD), bf16),
        vmem((blocks, keys, HD), bf16),
        vmem((blocks * tiles, keys, columns), f32), vmem((blocks * tiles, keys, columns), bf16),
        vmem((blocks * tiles, keys, columns), bf16),
        vmem((blocks * (topb + 1), BLK, HD), f32), vmem((blocks * (topb + 1), BLK, HD), f32),
        vmem(owned, f32), vmem(owned, f32),
        vmem(owned, bf16), vmem(owned, bf16), vmem(owned, bf16), vmem(owned, bf16),
        vmem(owned, bf16), vmem(owned, bf16),
        vmem((chips, tok, HD), bf16), vmem((chips, tok, HD), bf16),
        vmem((tok, width), bf16), vmem((2, tok, HD), bf16),
        pltpu.SMEM((1, 1, blocks, topb), jnp.int32),
        pltpu.SMEM((blocks * ctxs * blocks,), jnp.int32),
        pltpu.SemaphoreType.REGULAR,
        dma((7,)), dma, dma,
    ] + [dma((chips,)) for _ in range(16)]
    sizes = (pipes, ctxs, heads, tok, topb)
    hbm = pl.BlockSpec(memory_space=pltpu.HBM)
    results = (
        jax.ShapeDtypeStruct(queries.shape, bf16),
        jax.ShapeDtypeStruct(key_states.shape, bf16),
        jax.ShapeDtypeStruct(value_states.shape, bf16),
    )
    grads = pl.pallas_call(
        functools.partial(body, sizes),
        out_shape=results,
        in_specs=[hbm] * 5,
        out_specs=(hbm, hbm, hbm),
        scratch_shapes=scratch,
        compiler_params=pltpu.CompilerParams(
            collective_id=0, has_side_effects=True, vmem_limit_bytes=60 * 1024 * 1024
        ),
        name="selected_attention_grads",
    )(
        selected,
        queries,
        key_states.reshape(blocks, BLK, HD),
        value_states.reshape(blocks, BLK, HD),
        upstream,
    )
    return pl.pallas_call(
        hand_on,
        out_shape=results,
        in_specs=[hbm] * 3,
        out_specs=(hbm, hbm, hbm),
        scratch_shapes=[vmem(r.shape, r.dtype) for r in results] + [dma((3,)), dma((3,))],
        compiler_params=pltpu.CompilerParams(vmem_limit_bytes=60 * 1024 * 1024),
        name="hand_on_grads",
    )(*grads)


def solution(mesh):
    placed = (
        P("pipe", "ctx", "head"),
        P("pipe", "ctx", "head"),
        P("pipe", "ctx", "head"),
        P("pipe", ("ctx", "head"), None),
        P("pipe", "head", "ctx", None),
    )
    per = functools.partial(per_device, mesh.shape["pipe"], mesh.shape["ctx"], mesh.shape["head"])
    return jax.shard_map(
        per,
        mesh=mesh,
        in_specs=placed,
        out_specs=(P("pipe", "ctx", "head"), P("pipe", "ctx", "head"), P("pipe", "ctx", "head")),
        check_vma=False,
    )
```

```python
import functools

import jax
import jax.numpy as jnp
from jax import lax
from jax.experimental import pallas as pl
from jax.experimental.pallas import tpu as pltpu
from jax.sharding import PartitionSpec as P

HD = 128
BLK = 64
GROUP = 8
TILE_HEADS = 4
SCALE = HD ** (-0.5)
LOG2E = 1.4426950408889634

NT_DIMS = (((1,), (1,)), ((), ()))
TN_DIMS = (((0,), (0,)), ((), ()))


def rows_of(index, size):
    return pl.ds(pl.multiple_of(index * size, size), size)


def body(sizes, sel_in, q, k, v, up, dq_out, dk_out, dv_out, *scratch):
    pipes, ctxs, heads, tok, topb = sizes
    (
        kbuf, vbuf, qv, og, qs, os, ks, pf, pb, dsb, part_v, part_k,
        av, ak, sbv, sbk, rbv, rbk, gv, gk, hv, hk, sel, tbl, ready,
        loc_sem, up_send, up_recv,
        k_send, k_recv, k_fwd, k_sib, v_send, v_recv, v_fwd, v_sib,
        ev_send, ev_recv, ek_send, ek_recv,
        rv_send, rv_recv, rk_send, rk_recv,
    ) = scratch
    chips = ctxs // 2
    blocks = tok // BLK
    all_blocks = ctxs * blocks
    slots = topb + 1
    tiles = GROUP // TILE_HEADS
    width = GROUP * HD
    keys = topb * BLK
    up_rows = tok // heads

    z = lax.axis_index("pipe")
    c = lax.axis_index("ctx")
    y = lax.axis_index("head")
    x = c // 2
    core = c % 2
    other = c + 1 - 2 * core
    z_prev = (z + pipes - 1) % pipes
    z_next = (z + 1) % pipes

    def blocks_of(owner):
        return pl.ds(owner * blocks, blocks)

    def at_chip(chip):
        return (z, chip * 2 + core, y)

    sibling = (z, other, y)
    near_first = sorted(range(1, chips), key=lambda d: min(d, chips - d))

    def later_chips(step):
        for d in reversed(near_first):
            @pl.when(x + d < chips)
            def _(d=d):
                step(x + d)

    def earlier_chips(step, order):
        for d in order:
            @pl.when(x > d)
            def _(d=d):
                step(x - d)

        @pl.when(x > 0)
        def _():
            step(0)


    def remote(src, dst, send, recv, target):
        return pltpu.make_async_remote_copy(
            src_ref=src, dst_ref=dst, send_sem=send, recv_sem=recv,
            device_id=target, device_id_type=pl.DeviceIdType.MESH,
        )

    q_copy = pltpu.make_async_copy(q.at[0], qv, loc_sem.at[0])
    k_copy = pltpu.make_async_copy(k, kbuf.at[blocks_of(c)], loc_sem.at[1])
    v_copy = pltpu.make_async_copy(v, vbuf.at[blocks_of(c)], loc_sem.at[2])
    sel_copy = pltpu.make_async_copy(sel_in, sel, loc_sem.at[3])
    sel_copy.start()
    q_copy.start()
    k_copy.start()
    v_copy.start()

    barrier = pltpu.get_barrier_semaphore()

    def told_later(section):
        return jnp.logical_or(section == 0, jnp.logical_and(section == 1, c == 0))

    def as_int(flag):
        return jnp.where(flag, jnp.int32(1), jnp.int32(0))

    late = told_later(z)
    next_late = told_later(z_next)

    def greet(semaphore, target):
        pl.semaphore_signal(semaphore, inc=1, device_id=target, device_id_type=pl.DeviceIdType.MESH)

    def greet_chip(chip, carry):
        greet(barrier, at_chip(chip))
        return carry

    def greet_receiver(h, carry):
        greet(barrier, (z_prev, c, h))
        return carry

    def greet_sender(h, carry):
        greet(barrier, (z_next, c, h))
        return carry

    def tell_sender(h, carry):
        greet(ready, (z_next, c, h))
        return carry

    lax.fori_loop(0, x, greet_chip, 0)

    @pl.when(core == 1)
    def _():
        greet(barrier, sibling)

    @pl.when(jnp.logical_not(next_late))
    def _():
        lax.fori_loop(0, heads, greet_sender, 0)

    @pl.when(late)
    def _():
        lax.fori_loop(0, heads, greet_receiver, 0)

    expected = chips - 1 - x + (1 - core) + heads * (1 - as_int(late)) + heads * as_int(next_late)

    @pl.when(expected > 0)
    def _():
        pl.semaphore_wait(barrier, expected)

    def gather_copy(src, buf, send, recv, chip, target):
        return remote(src, buf.at[blocks_of(c)], send.at[chip], recv.at[x], target)

    def send_keys(chip):
        gather_copy(k, kbuf, k_send, k_recv, chip, at_chip(chip)).start()

    def send_values(chip):
        gather_copy(v, vbuf, v_send, v_recv, chip, at_chip(chip)).start()

    def send_to_sibling():
        gather_copy(k, kbuf, k_send, k_sib, x, sibling).start()
        gather_copy(v, vbuf, v_send, v_sib, x, sibling).start()

    def up_copy(h):
        return remote(
            up.at[0, :, rows_of(h, width)], og.at[rows_of(y, up_rows)],
            up_send, up_recv, (z_prev, c, h),
        )

    def send_up(h, carry):
        up_copy(h).start()
        return carry

    later_chips(send_keys)

    @pl.when(core == 0)
    def _():
        send_to_sibling()

    @pl.when(next_late)
    def _():
        lax.fori_loop(0, heads, tell_sender, 0)

    @pl.when(jnp.logical_not(late))
    def _():
        lax.fori_loop(0, heads, send_up, 0)

    sel_copy.wait()

    def slot_row(j, carry):
        for qb in range(blocks):
            slot = jnp.int32(topb)
            for t in range(topb):
                slot = jnp.where(sel[0, 0, qb, t] == j, jnp.int32(t), slot)
            tbl[qb * all_blocks + j] = slot + qb * slots
        return carry

    lax.fori_loop(0, all_blocks, slot_row, 0)
    zero_rows = jnp.zeros((BLK, HD), jnp.float32)
    for qb in range(blocks):
        part_v[qb * slots + topb] = zero_rows
        part_k[qb * slots + topb] = zero_rows

    def passed_on(buf, fwd, sib, chip):
        block = buf.at[blocks_of(chip * 2 + core)]
        return remote(block, block, fwd.at[chip], sib.at[chip], sibling)

    def arrived(buf, recv, chip):
        block = buf.at[blocks_of(chip * 2 + core)]
        return remote(block, block, recv.at[chip], recv.at[chip], sibling)

    def from_sibling(buf, sib, chip):
        block = buf.at[blocks_of(chip * 2 + 1 - core)]
        return remote(block, block, sib.at[chip], sib.at[chip], sibling)

    def forward_all(buf, recv, fwd, sib):
        def step(chip):
            arrived(buf, recv, chip).wait_recv()
            passed_on(buf, fwd, sib, chip).start()

        earlier_chips(step, near_first)

    def wait_sibling(buf, sib, count):
        def step(chip, carry):
            from_sibling(buf, sib, chip).wait_recv()
            return carry

        lax.fori_loop(0, count, step, 0)

    def key_left(chip):
        gather_copy(k, kbuf, k_send, k_recv, chip, at_chip(chip)).wait_send()

    @pl.when(x > 0)
    def _():
        later_chips(key_left)

    later_chips(send_values)

    @pl.when(core == 1)
    def _():
        from_sibling(kbuf, k_sib, x).wait_recv()
        send_to_sibling()

    forward_all(kbuf, k_recv, k_fwd, k_sib)
    q_copy.wait()
    k_copy.wait()
    v_copy.wait()
    wait_sibling(kbuf, k_sib, x + 1 - core)

    def chosen_rows(buf, qb):
        mine = c * blocks + qb
        return jnp.concatenate(
            [buf[jnp.minimum(sel[0, 0, qb, t], mine)] for t in range(topb)], axis=0
        )

    def head_rows(ref, qb, tile):
        return jnp.concatenate(
            [ref[rows_of(qb, BLK), rows_of(tile * TILE_HEADS + h, HD)] for h in range(TILE_HEADS)],
            axis=0,
        )

    columns = TILE_HEADS * BLK

    def score_step(i, carry):
        qb, tile = i // tiles, i % tiles
        mine = c * blocks + qb
        key_rows = chosen_rows(kbuf, qb)
        ks[qb] = key_rows
        query_rows = head_rows(qv, qb, tile)
        qs[i] = query_rows
        scores = lax.dot_general(key_rows, query_rows, NT_DIMS, preferred_element_type=jnp.float32)
        key_at = lax.broadcasted_iota(jnp.int32, (BLK, columns), 0)
        query_at = lax.broadcasted_iota(jnp.int32, (BLK, columns), 1) % BLK
        pieces = [jnp.where(key_at <= query_at, scores[:BLK], -jnp.inf)]
        for t in range(1, topb):
            shift = jnp.where(sel[0, 0, qb, t] > mine, jnp.float32(-jnp.inf), jnp.float32(0.0))
            pieces.append(scores[t * BLK:(t + 1) * BLK] + shift)
        scores = jnp.concatenate(pieces, axis=0)
        top = jnp.max(scores, axis=0, keepdims=True)
        weights = jnp.exp2((scores - top) * (SCALE * LOG2E))
        weights = weights * (1.0 / jnp.sum(weights, axis=0, keepdims=True))
        pf[i] = weights
        pb[i] = weights.astype(jnp.bfloat16)
        return carry

    lax.fori_loop(0, blocks * tiles, score_step, 0, unroll=True)

    all_up = remote(og, og, up_send, up_recv, sibling)
    all_up.wait_recv()

    def block_sums(lhs, rhs, part):
        def step(qb, carry):
            total = jnp.dot(lhs[qb * tiles], rhs[qb * tiles], preferred_element_type=jnp.float32)
            for tile in range(1, tiles):
                total += jnp.dot(
                    lhs[qb * tiles + tile], rhs[qb * tiles + tile], preferred_element_type=jnp.float32
                )
            for t in range(topb):
                part[qb * slots + t] = total[t * BLK:(t + 1) * BLK]
            return carry

        lax.fori_loop(0, blocks, step, 0, unroll=True)

    def grad_rows(i, carry):
        os[i] = head_rows(og, i // tiles, i % tiles)
        return carry

    lax.fori_loop(0, blocks * tiles, grad_rows, 0, unroll=True)
    block_sums(pb, os, part_v)

    half = chips // 2

    def farthest_first(count, step):
        def turn(i, carry):
            d = half + (1 - 2 * (i % 2)) * ((i + 1) // 2)

            @pl.when(x >= d)
            def _():
                step(x - d)

            return carry

        lax.fori_loop(0, count, turn, 0)

    def exchange_copy(src, dst, send, recv, chip):
        at = rows_of(chip, tok)
        return remote(src.at[at], dst.at[at], send.at[chip], recv.at[chip], sibling)

    def exchange(part, own, out, landing, send, recv):
        def owner_block(owner, b):
            j = owner * blocks + b
            total = part[tbl[j]]
            for qb in range(1, blocks):
                total = total + part[tbl[qb * all_blocks + j]]
            return total

        def step(chip):
            for b in range(blocks):
                at = rows_of(chip * blocks + b, BLK)
                out[at, :] = owner_block(chip * 2 + 1 - core, b).astype(jnp.bfloat16)
            exchange_copy(out, landing, send, recv, chip).start()
            for b in range(blocks):
                own[rows_of(chip * blocks + b, BLK), :] = owner_block(chip * 2 + core, b)

        farthest_first(chips, step)

    exchange(part_v, av, sbv, rbv, ev_send, ev_recv)

    def score_grad_step(i, carry):
        qb = i // tiles
        value_rows = chosen_rows(vbuf, qb)
        weight_grad = lax.dot_general(value_rows, os[i], NT_DIMS, preferred_element_type=jnp.float32)
        weights = pf[i]
        delta = jnp.sum(weights * weight_grad, axis=0, keepdims=True)
        dsb[i] = (weights * (weight_grad - delta) * SCALE).astype(jnp.bfloat16)
        return carry


    def owner_copy(src, dst, send, recv, chip):
        return remote(src.at[rows_of(chip, tok)], dst.at[x], send.at[chip], recv.at[x], at_chip(chip))

    def send_owned(own, src, landing, out, owners, send, landed, rsend, rrecv):
        def step(chip):
            at = rows_of(chip, tok)
            exchange_copy(src, landing, send, landed, chip).wait_recv()
            out[at, :] = (own[at, :] + landing[at, :].astype(jnp.float32)).astype(jnp.bfloat16)
            owner_copy(out, owners, rsend, rrecv, chip).start()

        farthest_first(chips - 1, step)
        at = rows_of(x, tok)
        exchange_copy(src, landing, send, landed, x).wait_recv()
        own[at, :] = own[at, :] + landing[at, :].astype(jnp.float32)

    send_owned(av, sbv, rbv, gv, hv, ev_send, ev_recv, rv_send, rv_recv)
    forward_all(vbuf, v_recv, v_fwd, v_sib)

    @pl.when(late)
    def _():
        pl.semaphore_wait(ready, heads)
        lax.fori_loop(0, heads, send_up, 0)


    wait_sibling(vbuf, v_sib, x + 1)
    lax.fori_loop(0, blocks * tiles, score_grad_step, 0, unroll=True)
    block_sums(dsb, qs, part_k)
    exchange(part_k, ak, sbk, rbk, ek_send, ek_recv)

    def query_step(i, carry):
        qb, tile = i // tiles, i % tiles
        grad = lax.dot_general(dsb[i], ks[qb], TN_DIMS, preferred_element_type=jnp.float32)
        grad = grad.astype(jnp.bfloat16)
        for h in range(TILE_HEADS):
            dq_out[0, rows_of(qb, BLK), rows_of(tile * TILE_HEADS + h, HD)] = grad[h * BLK:(h + 1) * BLK]
        return carry

    lax.fori_loop(0, blocks * tiles, query_step, 0, unroll=True)
    send_owned(ak, sbk, rbk, gk, hk, ek_send, ek_recv, rk_send, rk_recv)

    def left_gather(chip, carry):
        @pl.when(jnp.logical_or(chip == x, x == 0))
        def _():
            gather_copy(k, kbuf, k_send, k_recv, chip, at_chip(chip)).wait_send()

        gather_copy(v, vbuf, v_send, v_recv, chip, at_chip(chip)).wait_send()
        return carry

    def left_lower(chip, carry):
        passed_on(kbuf, k_fwd, k_sib, chip).wait_send()
        passed_on(vbuf, v_fwd, v_sib, chip).wait_send()
        owner_copy(gv, hv, rv_send, rv_recv, chip).wait_send()
        return carry

    def left_exchange(chip, carry):
        exchange_copy(sbv, rbv, ev_send, ev_recv, chip).wait_send()
        exchange_copy(sbk, rbk, ek_send, ek_recv, chip).wait_send()
        return carry

    lax.fori_loop(x, chips, left_gather, 0)
    all_up.wait_send()
    lax.fori_loop(0, x, left_lower, 0)
    lax.fori_loop(0, x + 1, left_exchange, 0)
    def owned_total(own, landing, recv, out):
        own_rows = own[rows_of(x, tok), :]

        def step(chip, total):
            block = landing.at[chip]
            remote(block, block, recv.at[chip], recv.at[chip], sibling).wait_recv()
            return total + landing[chip].astype(jnp.float32)

        out[0] = lax.fori_loop(x + 1, chips, step, own_rows).astype(jnp.bfloat16)

    owned_total(av, hv, rv_recv, dv_out)
    owned_total(ak, hk, rk_recv, dk_out)

    def left_owner_keys(chip, carry):
        owner_copy(gk, hk, rk_send, rk_recv, chip).wait_send()
        return carry

    lax.fori_loop(0, x, left_owner_keys, 0)


def hand_on(dq_in, dk_in, dv_in, dq_out, dk_out, dv_out, sems):
    pairs = ((dq_in, dq_out), (dk_in, dk_out), (dv_in, dv_out))
    copies = [pltpu.make_async_copy(a, b, sems.at[i]) for i, (a, b) in enumerate(pairs)]
    for copy in copies:
        copy.start()
    for copy in copies:
        copy.wait()


def per_device(pipes, ctxs, heads, queries, key_states, value_states, upstream, selected):
    tok = queries.shape[1]
    topb = selected.shape[3]
    blocks = tok // BLK
    chips = ctxs // 2
    tokens = tok * ctxs
    keys = topb * BLK
    tiles = GROUP // TILE_HEADS
    columns = TILE_HEADS * BLK
    width = GROUP * HD
    bf16, f32 = jnp.bfloat16, jnp.float32
    vmem = pltpu.VMEM
    dma = pltpu.SemaphoreType.DMA
    owned = (chips * tok, HD)
    scratch = [
        vmem((tokens // BLK, BLK, HD), bf16), vmem((tokens // BLK, BLK, HD), bf16),
        vmem((tok, width), bf16), vmem((tok, width), bf16),
        vmem((blocks * tiles, columns, HD), bf16), vmem((blocks * tiles, columns, HD), bf16),
        vmem((blocks, keys, HD), bf16),
        vmem((blocks * tiles, keys, columns), f32), vmem((blocks * tiles, keys, columns), bf16),
        vmem((blocks * tiles, keys, columns), bf16),
        vmem((blocks * (topb + 1), BLK, HD), f32), vmem((blocks * (topb + 1), BLK, HD), f32),
        vmem(owned, f32), vmem(owned, f32),
        vmem(owned, bf16), vmem(owned, bf16), vmem(owned, bf16), vmem(owned, bf16),
        vmem(owned, bf16), vmem(owned, bf16),
        vmem((chips, tok, HD), bf16), vmem((chips, tok, HD), bf16),
        pltpu.SMEM((1, 1, blocks, topb), jnp.int32),
        pltpu.SMEM((blocks * ctxs * blocks,), jnp.int32),
        pltpu.SemaphoreType.REGULAR,
        dma((7,)), dma, dma,
    ] + [dma((chips,)) for _ in range(16)]
    sizes = (pipes, ctxs, heads, tok, topb)
    hbm = pl.BlockSpec(memory_space=pltpu.HBM)
    whole = pl.BlockSpec(memory_space=pltpu.VMEM)
    results = (
        jax.ShapeDtypeStruct(queries.shape, bf16),
        jax.ShapeDtypeStruct(key_states.shape, bf16),
        jax.ShapeDtypeStruct(value_states.shape, bf16),
    )
    grads = pl.pallas_call(
        functools.partial(body, sizes),
        out_shape=tuple(vmem(r.shape, r.dtype) for r in results),
        in_specs=[hbm] * 5,
        out_specs=(whole, whole, whole),
        scratch_shapes=scratch,
        compiler_params=pltpu.CompilerParams(
            collective_id=0, has_side_effects=True, vmem_limit_bytes=60 * 1024 * 1024
        ),
        name="selected_attention_grads",
    )(
        selected,
        queries,
        key_states.reshape(blocks, BLK, HD),
        value_states.reshape(blocks, BLK, HD),
        upstream,
    )
    return pl.pallas_call(
        hand_on,
        out_shape=results,
        in_specs=[whole] * 3,
        out_specs=(hbm, hbm, hbm),
        scratch_shapes=[dma((3,))],
        compiler_params=pltpu.CompilerParams(vmem_limit_bytes=60 * 1024 * 1024),
        name="hand_on_grads",
    )(*[pltpu.with_memory_space_constraint(g, pltpu.VMEM) for g in grads])


def solution(mesh):
    placed = (
        P("pipe", "ctx", "head"),
        P("pipe", "ctx", "head"),
        P("pipe", "ctx", "head"),
        P("pipe", ("ctx", "head"), None),
        P("pipe", "head", "ctx", None),
    )
    per = functools.partial(per_device, mesh.shape["pipe"], mesh.shape["ctx"], mesh.shape["head"])
    return jax.shard_map(
        per,
        mesh=mesh,
        in_specs=placed,
        out_specs=(P("pipe", "ctx", "head"), P("pipe", "ctx", "head"), P("pipe", "ctx", "head")),
        check_vma=False,
    )
```

```python
import functools

import jax
import jax.numpy as jnp
from jax import lax
from jax.experimental import pallas as pl
from jax.experimental.pallas import tpu as pltpu
from jax.sharding import PartitionSpec as P

HD = 128
BLK = 64
GROUP = 8
TILE_HEADS = 4
SCALE = HD ** (-0.5)
LOG2E = 1.4426950408889634

NT_DIMS = (((1,), (1,)), ((), ()))
TN_DIMS = (((0,), (0,)), ((), ()))


def rows_of(index, size):
    return pl.ds(pl.multiple_of(index * size, size), size)


def body(sizes, sel_in, q, k, v, up, dq_out, dk_out, dv_out, *scratch):
    pipes, ctxs, heads, tok, topb = sizes
    (
        kbuf, vbuf, qv, og, qs, os, ks, pf, pb, dsb, part_v, part_k,
        av, ak, sbv, sbk, rbv, rbk, gv, gk, hv, hk, sel, tbl, ready,
        loc_sem, up_send, up_recv,
        k_send, k_recv, k_fwd, k_sib, v_send, v_recv, v_fwd, v_sib,
        ev_send, ev_recv, ek_send, ek_recv,
        rv_send, rv_recv, rk_send, rk_recv,
    ) = scratch
    chips = ctxs // 2
    blocks = tok // BLK
    all_blocks = ctxs * blocks
    slots = topb + 1
    tiles = GROUP // TILE_HEADS
    width = GROUP * HD
    keys = topb * BLK
    up_rows = tok // heads

    z = lax.axis_index("pipe")
    c = lax.axis_index("ctx")
    y = lax.axis_index("head")
    x = c // 2
    core = c % 2
    other = c + 1 - 2 * core
    z_prev = (z + pipes - 1) % pipes
    z_next = (z + 1) % pipes

    def blocks_of(owner):
        return pl.ds(owner * blocks, blocks)

    def at_chip(chip):
        return (z, chip * 2 + core, y)

    sibling = (z, other, y)
    near_first = sorted(range(1, chips), key=lambda d: min(d, chips - d))

    def later_chips(step):
        for d in reversed(near_first):
            @pl.when(x + d < chips)
            def _(d=d):
                step(x + d)

    def earlier_chips(step, order):
        for d in order:
            @pl.when(x > d)
            def _(d=d):
                step(x - d)

        @pl.when(x > 0)
        def _():
            step(0)


    def remote(src, dst, send, recv, target):
        return pltpu.make_async_remote_copy(
            src_ref=src, dst_ref=dst, send_sem=send, recv_sem=recv,
            device_id=target, device_id_type=pl.DeviceIdType.MESH,
        )

    q_copy = pltpu.make_async_copy(q.at[0], qv, loc_sem.at[0])
    k_copy = pltpu.make_async_copy(k, kbuf.at[blocks_of(c)], loc_sem.at[1])
    v_copy = pltpu.make_async_copy(v, vbuf.at[blocks_of(c)], loc_sem.at[2])
    sel_copy = pltpu.make_async_copy(sel_in, sel, loc_sem.at[3])
    sel_copy.start()
    q_copy.start()
    k_copy.start()
    v_copy.start()

    barrier = pltpu.get_barrier_semaphore()

    def told_later(section):
        return jnp.logical_or(section == 0, jnp.logical_and(section == 1, c == 0))

    def as_int(flag):
        return jnp.where(flag, jnp.int32(1), jnp.int32(0))

    late = told_later(z)
    next_late = told_later(z_next)

    def greet(semaphore, target):
        pl.semaphore_signal(semaphore, inc=1, device_id=target, device_id_type=pl.DeviceIdType.MESH)

    def greet_chip(chip, carry):
        greet(barrier, at_chip(chip))
        return carry

    def greet_receiver(h, carry):
        greet(barrier, (z_prev, c, h))
        return carry

    def greet_sender(h, carry):
        greet(barrier, (z_next, c, h))
        return carry

    def tell_sender(h, carry):
        greet(ready, (z_next, c, h))
        return carry

    lax.fori_loop(0, x, greet_chip, 0)

    @pl.when(core == 1)
    def _():
        greet(barrier, sibling)

    @pl.when(jnp.logical_not(next_late))
    def _():
        lax.fori_loop(0, heads, greet_sender, 0)

    @pl.when(late)
    def _():
        lax.fori_loop(0, heads, greet_receiver, 0)

    expected = chips - 1 - x + (1 - core) + heads * (1 - as_int(late)) + heads * as_int(next_late)

    @pl.when(expected > 0)
    def _():
        pl.semaphore_wait(barrier, expected)

    def gather_copy(src, buf, send, recv, chip, target):
        return remote(src, buf.at[blocks_of(c)], send.at[chip], recv.at[x], target)

    def send_keys(chip):
        gather_copy(k, kbuf, k_send, k_recv, chip, at_chip(chip)).start()

    def send_values(chip):
        gather_copy(v, vbuf, v_send, v_recv, chip, at_chip(chip)).start()

    def send_to_sibling():
        gather_copy(k, kbuf, k_send, k_sib, x, sibling).start()
        gather_copy(v, vbuf, v_send, v_sib, x, sibling).start()

    def up_copy(h):
        return remote(
            up.at[0, :, rows_of(h, width)], og.at[rows_of(y, up_rows)],
            up_send, up_recv, (z_prev, c, h),
        )

    def send_up(h, carry):
        up_copy(h).start()
        return carry

    later_chips(send_keys)

    @pl.when(core == 0)
    def _():
        send_to_sibling()

    @pl.when(next_late)
    def _():
        lax.fori_loop(0, heads, tell_sender, 0)

    @pl.when(jnp.logical_not(late))
    def _():
        lax.fori_loop(0, heads, send_up, 0)

    sel_copy.wait()

    def slot_row(j, carry):
        for qb in range(blocks):
            slot = jnp.int32(topb)
            for t in range(topb):
                slot = jnp.where(sel[0, 0, qb, t] == j, jnp.int32(t), slot)
            tbl[qb * all_blocks + j] = slot + qb * slots
        return carry

    lax.fori_loop(0, all_blocks, slot_row, 0)
    zero_rows = jnp.zeros((BLK, HD), jnp.float32)
    for qb in range(blocks):
        part_v[qb * slots + topb] = zero_rows
        part_k[qb * slots + topb] = zero_rows

    def passed_on(buf, fwd, sib, chip):
        block = buf.at[blocks_of(chip * 2 + core)]
        return remote(block, block, fwd.at[chip], sib.at[chip], sibling)

    def arrived(buf, recv, chip):
        block = buf.at[blocks_of(chip * 2 + core)]
        return remote(block, block, recv.at[chip], recv.at[chip], sibling)

    def from_sibling(buf, sib, chip):
        block = buf.at[blocks_of(chip * 2 + 1 - core)]
        return remote(block, block, sib.at[chip], sib.at[chip], sibling)

    def forward_all(buf, recv, fwd, sib):
        def step(chip):
            arrived(buf, recv, chip).wait_recv()
            passed_on(buf, fwd, sib, chip).start()

        earlier_chips(step, near_first)

    def wait_sibling(buf, sib, count):
        def step(chip, carry):
            from_sibling(buf, sib, chip).wait_recv()
            return carry

        lax.fori_loop(0, count, step, 0)

    def key_left(chip):
        gather_copy(k, kbuf, k_send, k_recv, chip, at_chip(chip)).wait_send()

    @pl.when(x > 0)
    def _():
        later_chips(key_left)

    later_chips(send_values)

    @pl.when(core == 1)
    def _():
        from_sibling(kbuf, k_sib, x).wait_recv()
        send_to_sibling()

    forward_all(kbuf, k_recv, k_fwd, k_sib)
    q_copy.wait()
    k_copy.wait()
    v_copy.wait()
    wait_sibling(kbuf, k_sib, x + 1 - core)

    def chosen_rows(buf, qb):
        mine = c * blocks + qb
        return jnp.concatenate(
            [buf[jnp.minimum(sel[0, 0, qb, t], mine)] for t in range(topb)], axis=0
        )

    def head_rows(ref, qb, tile):
        return jnp.concatenate(
            [ref[rows_of(qb, BLK), rows_of(tile * TILE_HEADS + h, HD)] for h in range(TILE_HEADS)],
            axis=0,
        )

    columns = TILE_HEADS * BLK

    def score_step(i, carry):
        qb, tile = i // tiles, i % tiles
        mine = c * blocks + qb
        key_rows = chosen_rows(kbuf, qb)
        ks[qb] = key_rows
        query_rows = head_rows(qv, qb, tile)
        qs[i] = query_rows
        scores = lax.dot_general(key_rows, query_rows, NT_DIMS, preferred_element_type=jnp.float32)
        key_at = lax.broadcasted_iota(jnp.int32, (BLK, columns), 0)
        query_at = lax.broadcasted_iota(jnp.int32, (BLK, columns), 1) % BLK
        pieces = [jnp.where(key_at <= query_at, scores[:BLK], -jnp.inf)]
        for t in range(1, topb):
            shift = jnp.where(sel[0, 0, qb, t] > mine, jnp.float32(-jnp.inf), jnp.float32(0.0))
            pieces.append(scores[t * BLK:(t + 1) * BLK] + shift)
        scores = jnp.concatenate(pieces, axis=0)
        top = jnp.max(scores, axis=0, keepdims=True)
        weights = jnp.exp2((scores - top) * (SCALE * LOG2E))
        weights = weights * (1.0 / jnp.sum(weights, axis=0, keepdims=True))
        pf[i] = weights
        pb[i] = weights.astype(jnp.bfloat16)
        return carry

    lax.fori_loop(0, blocks * tiles, score_step, 0, unroll=True)

    all_up = remote(og, og, up_send, up_recv, sibling)
    all_up.wait_recv()

    def block_sums(lhs, rhs, part):
        def step(qb, carry):
            total = jnp.dot(lhs[qb * tiles], rhs[qb * tiles], preferred_element_type=jnp.float32)
            for tile in range(1, tiles):
                total += jnp.dot(
                    lhs[qb * tiles + tile], rhs[qb * tiles + tile], preferred_element_type=jnp.float32
                )
            for t in range(topb):
                part[qb * slots + t] = total[t * BLK:(t + 1) * BLK]
            return carry

        lax.fori_loop(0, blocks, step, 0, unroll=True)

    def grad_rows(i, carry):
        os[i] = head_rows(og, i // tiles, i % tiles)
        return carry

    lax.fori_loop(0, blocks * tiles, grad_rows, 0, unroll=True)
    block_sums(pb, os, part_v)

    half = chips // 2

    def farthest_first(count, step):
        def turn(i, carry):
            d = half + (1 - 2 * (i % 2)) * ((i + 1) // 2)

            @pl.when(x >= d)
            def _():
                step(x - d)

            return carry

        lax.fori_loop(0, count, turn, 0)

    def exchange_copy(src, dst, send, recv, chip):
        at = rows_of(chip, tok)
        return remote(src.at[at], dst.at[at], send.at[chip], recv.at[chip], sibling)

    def exchange(part, own, out, landing, send, recv):
        def owner_block(owner, b):
            j = owner * blocks + b
            total = part[tbl[j]]
            for qb in range(1, blocks):
                total = total + part[tbl[qb * all_blocks + j]]
            return total

        def step(chip):
            for b in range(blocks):
                at = rows_of(chip * blocks + b, BLK)
                out[at, :] = owner_block(chip * 2 + 1 - core, b).astype(jnp.bfloat16)
            exchange_copy(out, landing, send, recv, chip).start()
            for b in range(blocks):
                own[rows_of(chip * blocks + b, BLK), :] = owner_block(chip * 2 + core, b)

        farthest_first(chips, step)

    exchange(part_v, av, sbv, rbv, ev_send, ev_recv)

    def score_grad_step(i, carry):
        qb = i // tiles
        value_rows = chosen_rows(vbuf, qb)
        weight_grad = lax.dot_general(value_rows, os[i], NT_DIMS, preferred_element_type=jnp.float32)
        weights = pf[i]
        delta = jnp.sum(weights * weight_grad, axis=0, keepdims=True)
        dsb[i] = (weights * (weight_grad - delta) * SCALE).astype(jnp.bfloat16)
        return carry


    def owner_copy(src, dst, send, recv, chip):
        return remote(src.at[rows_of(chip, tok)], dst.at[x], send.at[chip], recv.at[x], at_chip(chip))

    def send_owned(own, src, landing, out, owners, send, landed, rsend, rrecv):
        def step(chip):
            at = rows_of(chip, tok)
            exchange_copy(src, landing, send, landed, chip).wait_recv()
            out[at, :] = (own[at, :] + landing[at, :].astype(jnp.float32)).astype(jnp.bfloat16)
            owner_copy(out, owners, rsend, rrecv, chip).start()

        farthest_first(chips - 1, step)
        at = rows_of(x, tok)
        exchange_copy(src, landing, send, landed, x).wait_recv()
        own[at, :] = own[at, :] + landing[at, :].astype(jnp.float32)

    send_owned(av, sbv, rbv, gv, hv, ev_send, ev_recv, rv_send, rv_recv)
    forward_all(vbuf, v_recv, v_fwd, v_sib)

    @pl.when(late)
    def _():
        pl.semaphore_wait(ready, heads)
        lax.fori_loop(0, heads, send_up, 0)


    wait_sibling(vbuf, v_sib, x + 1)
    lax.fori_loop(0, blocks * tiles, score_grad_step, 0, unroll=True)
    block_sums(dsb, qs, part_k)
    exchange(part_k, ak, sbk, rbk, ek_send, ek_recv)

    def query_step(i, carry):
        qb, tile = i // tiles, i % tiles
        grad = lax.dot_general(dsb[i], ks[qb], TN_DIMS, preferred_element_type=jnp.float32)
        grad = grad.astype(jnp.bfloat16)
        for h in range(TILE_HEADS):
            dq_out[0, rows_of(qb, BLK), rows_of(tile * TILE_HEADS + h, HD)] = grad[h * BLK:(h + 1) * BLK]
        return carry

    send_owned(ak, sbk, rbk, gk, hk, ek_send, ek_recv, rk_send, rk_recv)
    lax.fori_loop(0, blocks * tiles, query_step, 0, unroll=True)

    def left_gather(chip, carry):
        @pl.when(jnp.logical_or(chip == x, x == 0))
        def _():
            gather_copy(k, kbuf, k_send, k_recv, chip, at_chip(chip)).wait_send()

        gather_copy(v, vbuf, v_send, v_recv, chip, at_chip(chip)).wait_send()
        return carry

    def left_lower(chip, carry):
        passed_on(kbuf, k_fwd, k_sib, chip).wait_send()
        passed_on(vbuf, v_fwd, v_sib, chip).wait_send()
        owner_copy(gv, hv, rv_send, rv_recv, chip).wait_send()
        return carry

    def left_exchange(chip, carry):
        exchange_copy(sbv, rbv, ev_send, ev_recv, chip).wait_send()
        exchange_copy(sbk, rbk, ek_send, ek_recv, chip).wait_send()
        return carry

    lax.fori_loop(x, chips, left_gather, 0)
    all_up.wait_send()
    lax.fori_loop(0, x, left_lower, 0)
    lax.fori_loop(0, x + 1, left_exchange, 0)
    def owned_total(own, landing, recv, out):
        own_rows = own[rows_of(x, tok), :]

        def step(chip, total):
            block = landing.at[chip]
            remote(block, block, recv.at[chip], recv.at[chip], sibling).wait_recv()
            return total + landing[chip].astype(jnp.float32)

        out[0] = lax.fori_loop(x + 1, chips, step, own_rows).astype(jnp.bfloat16)

    owned_total(av, hv, rv_recv, dv_out)
    owned_total(ak, hk, rk_recv, dk_out)

    def left_owner_keys(chip, carry):
        owner_copy(gk, hk, rk_send, rk_recv, chip).wait_send()
        return carry

    lax.fori_loop(0, x, left_owner_keys, 0)


def hand_on(dq_in, dk_in, dv_in, dq_out, dk_out, dv_out, sems):
    pairs = ((dq_in, dq_out), (dk_in, dk_out), (dv_in, dv_out))
    copies = [pltpu.make_async_copy(a, b, sems.at[i]) for i, (a, b) in enumerate(pairs)]
    for copy in copies:
        copy.start()
    for copy in copies:
        copy.wait()


def per_device(pipes, ctxs, heads, queries, key_states, value_states, upstream, selected):
    tok = queries.shape[1]
    topb = selected.shape[3]
    blocks = tok // BLK
    chips = ctxs // 2
    tokens = tok * ctxs
    keys = topb * BLK
    tiles = GROUP // TILE_HEADS
    columns = TILE_HEADS * BLK
    width = GROUP * HD
    bf16, f32 = jnp.bfloat16, jnp.float32
    vmem = pltpu.VMEM
    dma = pltpu.SemaphoreType.DMA
    owned = (chips * tok, HD)
    scratch = [
        vmem((tokens // BLK, BLK, HD), bf16), vmem((tokens // BLK, BLK, HD), bf16),
        vmem((tok, width), bf16), vmem((tok, width), bf16),
        vmem((blocks * tiles, columns, HD), bf16), vmem((blocks * tiles, columns, HD), bf16),
        vmem((blocks, keys, HD), bf16),
        vmem((blocks * tiles, keys, columns), f32), vmem((blocks * tiles, keys, columns), bf16),
        vmem((blocks * tiles, keys, columns), bf16),
        vmem((blocks * (topb + 1), BLK, HD), f32), vmem((blocks * (topb + 1), BLK, HD), f32),
        vmem(owned, f32), vmem(owned, f32),
        vmem(owned, bf16), vmem(owned, bf16), vmem(owned, bf16), vmem(owned, bf16),
        vmem(owned, bf16), vmem(owned, bf16),
        vmem((chips, tok, HD), bf16), vmem((chips, tok, HD), bf16),
        pltpu.SMEM((1, 1, blocks, topb), jnp.int32),
        pltpu.SMEM((blocks * ctxs * blocks,), jnp.int32),
        pltpu.SemaphoreType.REGULAR,
        dma((7,)), dma, dma,
    ] + [dma((chips,)) for _ in range(16)]
    sizes = (pipes, ctxs, heads, tok, topb)
    hbm = pl.BlockSpec(memory_space=pltpu.HBM)
    whole = pl.BlockSpec(memory_space=pltpu.VMEM)
    results = (
        jax.ShapeDtypeStruct(queries.shape, bf16),
        jax.ShapeDtypeStruct(key_states.shape, bf16),
        jax.ShapeDtypeStruct(value_states.shape, bf16),
    )
    grads = pl.pallas_call(
        functools.partial(body, sizes),
        out_shape=tuple(vmem(r.shape, r.dtype) for r in results),
        in_specs=[hbm] * 5,
        out_specs=(whole, whole, whole),
        scratch_shapes=scratch,
        compiler_params=pltpu.CompilerParams(
            collective_id=0, has_side_effects=True, vmem_limit_bytes=60 * 1024 * 1024
        ),
        name="selected_attention_grads",
    )(
        selected,
        queries,
        key_states.reshape(blocks, BLK, HD),
        value_states.reshape(blocks, BLK, HD),
        upstream,
    )
    return pl.pallas_call(
        hand_on,
        out_shape=results,
        in_specs=[whole] * 3,
        out_specs=(hbm, hbm, hbm),
        scratch_shapes=[dma((3,))],
        compiler_params=pltpu.CompilerParams(vmem_limit_bytes=60 * 1024 * 1024),
        name="hand_on_grads",
    )(*[pltpu.with_memory_space_constraint(g, pltpu.VMEM) for g in grads])


def solution(mesh):
    placed = (
        P("pipe", "ctx", "head"),
        P("pipe", "ctx", "head"),
        P("pipe", "ctx", "head"),
        P("pipe", ("ctx", "head"), None),
        P("pipe", "head", "ctx", None),
    )
    per = functools.partial(per_device, mesh.shape["pipe"], mesh.shape["ctx"], mesh.shape["head"])
    return jax.shard_map(
        per,
        mesh=mesh,
        in_specs=placed,
        out_specs=(P("pipe", "ctx", "head"), P("pipe", "ctx", "head"), P("pipe", "ctx", "head")),
        check_vma=False,
    )
```
